32 devices in a mesh: dp: 8 (over y, x, core), ffn: 4 (over z).
Axes of the slice: x: 2, y: 2, z: 4, core: 2. Of those that a mesh axis runs over, the one named last changes fastest.
Arguments:
- seg_input: bfloat16 [2, 8, 512, 1024], P(None, 'dp', 'ffn'), may hold values from -6 to 6
- memory: bfloat16 [2, 8, 384, 1024], P(None, 'dp', 'ffn'), may hold values from -6 to 6
- compressed: bfloat16 [2, 8, 512, 1024], P(None, 'dp', 'ffn'), may hold values from -6 to 6
- mem_fill: int32 [2, 8], P(None, 'dp'), may hold values from 0 to 384, as said below
- comp_fill: int32 [2, 8], P(None, 'dp'), may hold values from 0 to 512, as said below
- attn_gain: float32 [1024], replicated, may hold values from 0.5 to 1.5
- attn_shift: float32 [1024], replicated, may hold values from -1.75 to 1.75
- attn_weights: bfloat16 [4096, 1024], replicated, may hold values from -1.5 to 1.5
- rel_table: float32 [8, 22], replicated, may hold values from -6 to 6
- ffn_gain: float32 [1024], replicated, may hold values from 0.5 to 1.5
- ffn_shift: float32 [1024], replicated, may hold values from -1.75 to 1.75
- w_up: bfloat16 [1024, 4096], P(None, 'ffn'), may hold values from -0.1875 to 0.1875
- b_up: float32 [4096], P('ffn'), may hold values from -1.75 to 1.75
- w_down: bfloat16 [4096, 1024], P('ffn'), may hold values from -0.125 to 0.125
- b_down: float32 [1024], replicated, may hold values from -1.75 to 1.75
- conv_weight: bfloat16 [3072, 1024], replicated, may hold values from -0.109375 to 0.109375
- conv_bias: float32 [1024], replicated, may hold values from -1.75 to 1.75
- out_grad: bfloat16 [2, 8, 512, 1024], P(None, 'dp', 'ffn'), may hold values from -6 to 6
- comp_grad: bfloat16 [2, 8, 128, 1024], P(None, 'dp', 'ffn'), may hold values from -6 to 6
Outputs:
- layer_out: bfloat16 [2, 8, 512, 1024], P(None, 'dp', 'ffn')
- new_compressed: bfloat16 [2, 8, 128, 1024], P(None, 'dp', 'ffn')
- seg_grad: float32 [2, 8, 512, 1024], P(None, 'dp', 'ffn')
- attn_gain_grad: float32 [1024], replicated
- attn_shift_grad: float32 [1024], replicated
- attn_weights_grad: float32 [4096, 1024], P(('dp', 'ffn'))
- rel_table_grad: float32 [8, 22], replicated
- ffn_gain_grad: float32 [1024], replicated
- ffn_shift_grad: float32 [1024], replicated
- w_up_grad: float32 [1024, 4096], P('dp', 'ffn')
- b_up_grad: float32 [4096], replicated
- w_down_grad: float32 [4096, 1024], P('ffn', 'dp')
- b_down_grad: float32 [1024], replicated
- conv_weight_grad: float32 [3072, 1024], replicated
- conv_bias_grad: float32 [1024], replicated
The draws below stay inside these ranges and needn't reach their ends.
Inputs may be any that keep to these rules, and one draw needn't show every extreme that they name: `mem_fill`: in every micro-batch one stream has all 384 memory slots live and another none; live slots are the newest, at the end of the buffer. `comp_fill`: in every micro-batch one stream has all 512 compressed slots live and another none; live slots are the newest, at the end of the buffer.
All inputs are finite; a program needn't handle non-finite values.
Results may differ from the reference program's by a relative error of at most 0.028.
Values may be sent and summed in bfloat16 or wider, within the bound.
No kernel may reach another device: no remote copies, remote signals or barrier semaphores. Data moves between devices by JAX's collectives and lax.ppermute only.
A program may use at most 320 MiB of HBM per device.

```python
import math
import jax
import jax.numpy as jnp
from jax import lax

D = 1024
H = 8
HD = 128
FF = 4096
MICRO = 2
SEG = 512
M = 384
CM = 512
PW = 64
KR = 1408
NB = 22
STREAMS = 8


def fill_counts(key, most):
    counts = jax.random.randint(key, (MICRO, STREAMS), 0, most + 1)
    full_stream = jax.random.randint(jax.random.fold_in(key, 7), (MICRO, 1), 0, STREAMS)
    empty_stream = (full_stream + 1) % STREAMS
    column = jnp.arange(STREAMS, dtype=jnp.int32)[None, :]
    counts = jnp.where(column == full_stream, most, counts)
    return jnp.where(column == empty_stream, 0, counts).astype(jnp.int32)


def draw_mem_fill(key, part):
    return fill_counts(jax.random.fold_in(key, 11), M)


def draw_comp_fill(key, part):
    return fill_counts(jax.random.fold_in(key, 23), CM)


def draw_attn_weights(key, part):
    entries = jnp.clip(jax.random.normal(jax.random.fold_in(key, 37), (4 * D, D), jnp.float32), -6.0, 6.0)
    row_ids = jnp.arange(4 * D, dtype=jnp.int32)[:, None]
    factor = jnp.where(row_ids < 3 * D, 1.0, 8.0) / math.sqrt(D)
    return (entries * factor).astype(jnp.bfloat16)


def levels(own_key, dims, pieces, smallest, top_value):
    level, own = 1.0, jax.random.fold_in(own_key, 6)
    for dim, blocks in pieces:
        steps = jnp.exp(jax.random.uniform(jax.random.fold_in(own, dim), (blocks,), jnp.float32, smallest / len(pieces), top_value / len(pieces)))
        level = level * jnp.repeat(steps, dims[dim] // blocks).reshape([-1 if axis == dim else 1 for axis in range(len(dims))])
    return level


def bell_draw(rng, extent, spread, most, shards=(), kind=jnp.bfloat16):
    factor_of = levels(rng, extent, shards, -0.22, 0.18) if shards else 1.0
    result = jax.random.normal(rng, extent, jnp.float32) * spread * factor_of
    return jnp.minimum(jnp.maximum(result, -most), most).astype(kind)


def setup_inputs(seed: int = 0) -> dict:
    streams_of = jax.random.split(jax.random.key(seed), 20)
    seg_input = bell_draw(streams_of[0], (MICRO, STREAMS, SEG, D), 1.0, 6.0, ((1, 8), (2, 4)))
    memory = bell_draw(streams_of[1], (MICRO, STREAMS, M, D), 1.0, 6.0, ((1, 8), (2, 4)))
    compressed = bell_draw(streams_of[2], (MICRO, STREAMS, CM, D), 1.0, 6.0, ((1, 8), (2, 4)))
    mem_fill = draw_mem_fill(jax.random.fold_in(streams_of[19], 71), 0)
    comp_fill = draw_comp_fill(jax.random.fold_in(streams_of[19], 71), 0)
    attn_gain = jnp.clip(1.0 + 0.1 * jax.random.normal(streams_of[5], (D,), jnp.float32), 0.5, 1.5)
    attn_shift = bell_draw(streams_of[6], (D,), 0.3, 1.75, (), jnp.float32)
    attn_weights = draw_attn_weights(jax.random.fold_in(streams_of[19], 71), 0)
    rel_table = bell_draw(streams_of[8], (H, NB), 1.0, 6.0, (), jnp.float32)
    ffn_gain = jnp.clip(1.0 + 0.1 * jax.random.normal(streams_of[9], (D,), jnp.float32), 0.5, 1.5)
    ffn_shift = bell_draw(streams_of[10], (D,), 0.3, 1.75, (), jnp.float32)
    w_up = bell_draw(streams_of[11], (D, FF), D ** -0.5, 0.1875, ((1, 4),))
    b_up = bell_draw(streams_of[12], (FF,), 0.3, 1.75, ((0, 4),), jnp.float32)
    w_down = bell_draw(streams_of[13], (FF, D), (FF // 2) ** -0.5, 0.125, ((0, 4),))
    b_down = bell_draw(streams_of[14], (D,), 0.3, 1.75, (), jnp.float32)
    conv_weight = bell_draw(streams_of[15], (3 * D, D), (3 * D) ** -0.5, 0.109375)
    conv_bias = bell_draw(streams_of[16], (D,), 0.3, 1.75, (), jnp.float32)
    out_grad = bell_draw(streams_of[17], (MICRO, STREAMS, SEG, D), 1.0, 6.0, ((1, 8), (2, 4)))
    comp_grad = bell_draw(streams_of[18], (MICRO, STREAMS, M // 3, D), 1.0, 6.0, ((1, 8), (2, 4)))
    return dict(seg_input=seg_input, memory=memory, compressed=compressed, mem_fill=mem_fill, comp_fill=comp_fill, attn_gain=attn_gain, attn_shift=attn_shift, attn_weights=attn_weights, rel_table=rel_table, ffn_gain=ffn_gain, ffn_shift=ffn_shift, w_up=w_up, b_up=b_up, w_down=w_down, b_down=b_down, conv_weight=conv_weight, conv_bias=conv_bias, out_grad=out_grad, comp_grad=comp_grad)


@jax.custom_vjp
def low(v):
    return lax.optimization_barrier(v.astype(jnp.bfloat16)).astype(jnp.float32)

@jax.custom_vjp
def low_back(v):
    return v

def low_keep(v):
    return (low(v), None)

def low_pass(kept, grad):
    return (grad,)

def back_keep(v):
    return (v, None)

def back_low(kept, grad):
    return (low(grad),)
low.defvjp(low_keep, low_pass)
low_back.defvjp(back_keep, back_low)

def normalize(rows_in, gain, shift):
    centre = lax.optimization_barrier(jnp.mean(rows_in, axis=-1, keepdims=True))
    centred = rows_in - centre
    variance = lax.optimization_barrier(jnp.mean(centred * centred, axis=-1, keepdims=True))
    return centred * lax.rsqrt(variance + 1e-05) * gain + shift

def matmul(left, right):
    return jnp.dot(left, right, precision=lax.Precision.HIGHEST)

def forward(params, segment, memory_rows, compressed_rows, mem_count, comp_count):
    norm_gain, norm_shift, weights_all, rel_bias, ffn_gain, ffn_shift, up_weight, up_bias, down_weight, down_bias, conv_kernel, conv_shift = params
    source = jnp.concatenate([compressed_rows, memory_rows, segment], axis=0)
    normed = low(normalize(source, norm_gain, norm_shift))
    queries = low(low_back(matmul(normed[CM + M:], weights_all[:D]))).reshape(SEG, H, HD)
    key_heads = low(low_back(matmul(normed, weights_all[D:2 * D]))).reshape(KR, H, HD)
    values = low(low_back(matmul(normed, weights_all[2 * D:3 * D]))).reshape(KR, H, HD)
    key_pos = jnp.arange(KR, dtype=jnp.int32)
    query_pos = CM + M + jnp.arange(SEG, dtype=jnp.int32)
    bucket = jnp.clip(query_pos[:, None] // PW - key_pos[None, :] // PW, 0, NB - 1)
    raw_scores = jnp.einsum('qhd,khd->hqk', queries, key_heads, precision=lax.Precision.HIGHEST) * HD ** (-0.5)
    raw_scores = low_back(raw_scores + rel_bias[:, bucket])
    live_keys = jnp.where(key_pos < CM, key_pos >= CM - comp_count, jnp.where(key_pos < CM + M, key_pos >= CM + M - mem_count, True))
    key_mask = live_keys[None, :] & (key_pos[None, :] <= query_pos[:, None])
    masked = jnp.where(key_mask[None], raw_scores, -1e+30)
    attention = low(jax.nn.softmax(masked, axis=-1))
    mixed_heads = jnp.einsum('hqk,khd->qhd', attention, values, precision=lax.Precision.HIGHEST).reshape(SEG, D)
    mixed_heads = low(low_back(mixed_heads))
    residual = segment + low_back(matmul(mixed_heads, weights_all[3 * D:]))
    ffn_in = low(normalize(residual, ffn_gain, ffn_shift))
    activated = low(jax.nn.gelu(low_back(matmul(ffn_in, up_weight) + up_bias), approximate=False))
    layer_rows = residual + low_back(matmul(activated, down_weight) + down_bias)
    alive_rows = jnp.arange(M, dtype=jnp.int32) >= M - mem_count
    flat_memory = jnp.where(alive_rows[:, None], memory_rows, 0.0).reshape(M // 3, 3 * D)
    compressed_new = matmul(flat_memory, conv_kernel) + conv_shift
    return (layer_rows, compressed_new)

def reference(seg_input, memory, compressed, mem_fill, comp_fill, attn_gain, attn_shift, attn_weights, rel_table, ffn_gain, ffn_shift, w_up, b_up, w_down, b_down, conv_weight, conv_bias, out_grad, comp_grad):
    params = tuple((entry.astype(jnp.float32) for entry in (attn_gain, attn_shift, attn_weights, rel_table, ffn_gain, ffn_shift, w_up, b_up, w_down, b_down, conv_weight, conv_bias)))
    streams_all = MICRO * STREAMS
    samples = (seg_input.reshape(streams_all, SEG, D), memory.reshape(streams_all, M, D), compressed.reshape(streams_all, CM, D), mem_fill.reshape(streams_all), comp_fill.reshape(streams_all), out_grad.reshape(streams_all, SEG, D), comp_grad.reshape(streams_all, M // 3, D))

    def per_stream(totals, sample):
        segment, memory_rows, compressed_rows, mem_count, comp_count, grad_rows, comp_cot = sample

        def forward_one(pars, rows_in):
            return forward(pars, rows_in, memory_rows.astype(jnp.float32), compressed_rows.astype(jnp.float32), mem_count, comp_count)
        outputs, pullback = jax.vjp(forward_one, params, segment.astype(jnp.float32))
        gradients, grad_segment = pullback((grad_rows.astype(jnp.float32), comp_cot.astype(jnp.float32)))
        totals = jax.tree.map(jnp.add, totals, gradients)
        return (totals, (outputs[0].astype(jnp.bfloat16), outputs[1].astype(jnp.bfloat16), grad_segment))
    zero_grads = jax.tree.map(jnp.zeros_like, params)
    totals, stacked = lax.scan(per_stream, zero_grads, samples)
    layer_all = stacked[0].reshape(MICRO, STREAMS, SEG, D)
    compressed_all = stacked[1].reshape(MICRO, STREAMS, M // 3, D)
    grad_all = stacked[2].reshape(MICRO, STREAMS, SEG, D)
    return (layer_all, compressed_all, grad_all, totals[0], totals[1], totals[2], totals[3], totals[4], totals[5], totals[6], totals[7], totals[8], totals[9], totals[10], totals[11])
```

```python
import functools
import math

import jax
import jax.numpy as jnp
from jax import lax
from jax.experimental import pallas as pl
from jax.experimental.pallas import tpu as pltpu
from jax.sharding import PartitionSpec as P

D = 1024
H = 8
HD = 128
SEG = 512
M = 384
CM = 512
PW = 64
KR = 1408
NB = 22
OH = 4
HALF = OH * HD
EPSILON = 1e-05
MASKED = -1e30
SCALE = HD ** (-0.5)
BF = jnp.bfloat16
F32 = jnp.float32


def statistics(rows_in):
    centre = jnp.mean(rows_in, axis=-1, keepdims=True)
    centred = rows_in - centre
    variance = jnp.mean(centred * centred, axis=-1, keepdims=True)
    inverse = lax.rsqrt(variance + EPSILON)
    return centred * inverse, inverse


def matmul(left, right):
    return jnp.dot(left, right, preferred_element_type=F32)


def contract_rows(left, right):
    return lax.dot_general(left, right, (((0,), (0,)), ((), ())), preferred_element_type=F32)


def times_transposed(left, right):
    return lax.dot_general(left, right, (((1,), (1,)), ((), ())), preferred_element_type=F32)


def norm_pull(xhat, inverse, scaled):
    mean_a = jnp.mean(scaled, axis=-1, keepdims=True)
    mean_b = jnp.mean(scaled * xhat, axis=-1, keepdims=True)
    return (scaled - mean_a - xhat * mean_b) * inverse


def attention_forward_kernel(counts, q_ref, k_ref, v_ref, bias_ref, o_ref, p_ref):
    comp_low = CM - counts[0]
    mem_low = CM + M - counts[1]
    for tile in range(SEG // HD):
        cols = slice(tile * HD, (tile + 1) * HD)
        seen = CM + M + (tile + 1) * HD
        raw = times_transposed(k_ref[:seen, :], q_ref[cols, :]) * SCALE
        blocks = seen // PW
        raw = (
            raw.reshape(blocks, PW, HD) + bias_ref[0, :blocks, cols].reshape(blocks, 1, HD)
        ).reshape(seen, HD)
        key_pos = lax.broadcasted_iota(jnp.int32, (seen, HD), 0)
        query_pos = CM + M + tile * HD + lax.broadcasted_iota(jnp.int32, (seen, HD), 1)
        low = jnp.where(key_pos < CM, comp_low, jnp.where(key_pos < CM + M, mem_low, 0))
        scores = jnp.where((key_pos >= low) & (key_pos <= query_pos), raw, MASKED)
        top = jnp.max(scores, axis=0, keepdims=True)
        expanded = jnp.exp(scores - top)
        total = jnp.sum(expanded, axis=0, keepdims=True)
        attention = (expanded * (1.0 / total)).astype(BF)
        p_ref[0, :seen, cols] = attention
        if seen < KR:
            p_ref[0, seen:, cols] = jnp.zeros((KR - seen, HD), BF)
        mixed = contract_rows(v_ref[:seen, :], attention)
        o_ref[cols, :] = mixed.T.astype(BF)


def attention_forward(counts, queries, keys, values, bias):
    return pl.pallas_call(
        attention_forward_kernel,
        grid=(OH,),
        in_specs=[
            pl.BlockSpec(memory_space=pltpu.SMEM),
            pl.BlockSpec((SEG, HD), lambda h: (0, h)),
            pl.BlockSpec((KR, HD), lambda h: (0, h)),
            pl.BlockSpec((KR, HD), lambda h: (0, h)),
            pl.BlockSpec((1, NB, SEG), lambda h: (h, 0, 0)),
        ],
        out_specs=[
            pl.BlockSpec((SEG, HD), lambda h: (0, h)),
            pl.BlockSpec((1, KR, SEG), lambda h: (h, 0, 0)),
        ],
        out_shape=[
            jax.ShapeDtypeStruct((SEG, HALF), BF),
            jax.ShapeDtypeStruct((OH, KR, SEG), BF),
        ],
        cost_estimate=pl.CostEstimate(
            flops=4 * OH * SEG * KR * HD, bytes_accessed=10 << 20, transcendentals=OH * SEG * KR
        ),
        name="attention_forward",
    )(counts, queries, keys, values, bias)


def attention_backward_kernel(
    p_ref, q_ref, k_ref, v_ref, g_ref, dq_ref, dk_ref, dv_ref, sums_ref, ds_ref
):
    for tile in range(SEG // HD):
        cols = slice(tile * HD, (tile + 1) * HD)
        seen = CM + M + (tile + 1) * HD
        blocks = seen // PW
        attention = p_ref[0, :seen, cols].astype(F32)
        grad_attention = times_transposed(v_ref[:seen, :], g_ref[cols, :])
        inner = jnp.sum(attention * grad_attention, axis=0, keepdims=True)
        grad_scores = (attention * (grad_attention - inner)).astype(BF)
        ds_ref[:seen, cols] = grad_scores
        sums_ref[0, :blocks, cols] = jnp.sum(
            grad_scores.astype(F32).reshape(blocks, PW, HD), axis=1
        )
        if seen < KR:
            ds_ref[seen:, cols] = jnp.zeros((KR - seen, HD), BF)
            sums_ref[0, blocks:, cols] = jnp.zeros((NB - blocks, HD), F32)
        grad_query = contract_rows(k_ref[:seen, :], grad_scores) * SCALE
        dq_ref[cols, :] = grad_query.T.astype(BF)
    dk_ref[...] = (matmul(ds_ref[...], q_ref[...]) * SCALE).astype(BF)
    dv_ref[...] = matmul(p_ref[0], g_ref[...]).astype(BF)


def attention_backward(attention, queries, keys, values, grad_mixed):
    rows_of = lambda n: pl.BlockSpec((n, HD), lambda h: (0, h))
    return pl.pallas_call(
        attention_backward_kernel,
        grid=(OH,),
        in_specs=[
            pl.BlockSpec((1, KR, SEG), lambda h: (h, 0, 0)),
            rows_of(SEG),
            rows_of(KR),
            rows_of(KR),
            rows_of(SEG),
        ],
        out_specs=[
            rows_of(SEG),
            rows_of(KR),
            rows_of(KR),
            pl.BlockSpec((1, NB, SEG), lambda h: (h, 0, 0)),
        ],
        out_shape=[
            jax.ShapeDtypeStruct((SEG, HALF), BF),
            jax.ShapeDtypeStruct((KR, HALF), BF),
            jax.ShapeDtypeStruct((KR, HALF), BF),
            jax.ShapeDtypeStruct((OH, NB, SEG), F32),
        ],
        scratch_shapes=[pltpu.VMEM((KR, SEG), BF)],
        cost_estimate=pl.CostEstimate(
            flops=8 * OH * SEG * KR * HD, bytes_accessed=14 << 20, transcendentals=0
        ),
        name="attention_backward",
    )(attention, queries, keys, values, grad_mixed)


def feed_forward_kernel(
    place, x_ref, gy_ref, up_ref, bias_ref, down_ref, res_ref,
    part_ref, grad_ref, sum_ref, weights_ref, up_acc, down_acc,
):
    block = pl.program_id(0)
    rows = x_ref[0]
    gy = gy_ref[0]
    hidden = matmul(rows, up_ref[...]) + bias_ref[...]
    normal = 0.5 * (1.0 + lax.erf(hidden * math.sqrt(0.5)))
    slope = normal + hidden * jnp.exp(-0.5 * hidden * hidden) * (1.0 / math.sqrt(2.0 * math.pi))
    activated = (hidden * normal).astype(BF)
    part = matmul(activated, down_ref[...])
    own = (block == place[0]).astype(F32)
    part_ref[0] = (part + own * res_ref[...]).astype(BF)
    grad_hidden = times_transposed(gy, down_ref[...])
    grad_pre = (grad_hidden * slope).astype(BF)
    grad_ref[0] = times_transposed(grad_pre, up_ref[...]).astype(BF)
    column_sum = jnp.sum(grad_pre.astype(F32), axis=0, keepdims=True)
    up_part = contract_rows(rows, grad_pre)
    down_part = contract_rows(gy, activated)

    @pl.when(block == 0)
    def _():
        sum_ref[...] = column_sum
        up_acc[...] = up_part
        down_acc[...] = down_part

    @pl.when(block > 0)
    def _():
        sum_ref[...] += column_sum
        up_acc[...] += up_part
        down_acc[...] += down_part

    @pl.when(block == pl.num_programs(0) - 1)
    def _():
        pieces, _, height, _ = weights_ref.shape
        for piece in range(pieces):
            span = slice(piece * height, (piece + 1) * height)
            weights_ref[piece, 0] = up_acc[span, :].astype(BF)
            weights_ref[piece, 1] = down_acc[span, :].astype(BF)


def feed_forward(place, rows, gy, w_up, b_up, w_down, residual, pieces):
    blocks, height, _ = rows.shape
    hidden = w_up.shape[1]
    whole = lambda a, b: pl.BlockSpec((a, b), lambda i: (0, 0))
    each = pl.BlockSpec((1, height, D), lambda i: (i, 0, 0))
    return pl.pallas_call(
        feed_forward_kernel,
        grid=(blocks,),
        in_specs=[
            pl.BlockSpec(memory_space=pltpu.SMEM),
            each,
            each,
            whole(D, hidden),
            whole(1, hidden),
            whole(hidden, D),
            whole(height, D),
        ],
        out_specs=[
            each,
            each,
            whole(1, hidden),
            pl.BlockSpec((pieces, 2, D // pieces, hidden), lambda i: (0, 0, 0, 0)),
        ],
        out_shape=[
            jax.ShapeDtypeStruct((blocks, height, D), BF),
            jax.ShapeDtypeStruct((blocks, height, D), BF),
            jax.ShapeDtypeStruct((1, hidden), F32),
            jax.ShapeDtypeStruct((pieces, 2, D // pieces, hidden), BF),
        ],
        scratch_shapes=[pltpu.VMEM((D, hidden), F32), pltpu.VMEM((D, hidden), F32)],
        compiler_params=pltpu.CompilerParams(vmem_limit_bytes=60 << 20),
        cost_estimate=pl.CostEstimate(
            flops=12 * blocks * height * D * hidden,
            bytes_accessed=20 << 20,
            transcendentals=2 * blocks * height * hidden,
        ),
        name="feed_forward",
    )(place, rows, gy, w_up, b_up.reshape(1, hidden), w_down, residual)


def on_device(
    seg_input,
    memory,
    compressed,
    mem_fill,
    comp_fill,
    attn_gain,
    attn_shift,
    attn_weights,
    rel_table,
    ffn_gain,
    ffn_shift,
    w_up,
    b_up,
    w_down,
    b_down,
    conv_weight,
    conv_bias,
    out_grad,
    comp_grad,
):
    streams = lax.axis_size("dp")
    layers = lax.axis_size("ffn")
    stream = lax.axis_index("dp")
    layer = lax.axis_index("ffn")
    core = stream % 2
    micros = seg_input.shape[0]
    seg_rows, mem_rows, comp_rows = seg_input.shape[2], memory.shape[2], compressed.shape[2]
    hidden_local = w_up.shape[1]
    groups = streams // 2
    twins = [(i, i ^ 1) for i in range(streams)]
    first = core == 0

    def swap(value):
        return lax.ppermute(value, "dp", twins)

    def by_core(mine, other, axis):
        return jnp.where(
            first, jnp.stack([mine, other], axis=axis), jnp.stack([other, mine], axis=axis)
        )

    def halves(value):
        split = value.reshape(micros, 2, value.shape[1] // 2, D)
        return (
            lax.dynamic_index_in_dim(split, core, 1, keepdims=False),
            lax.dynamic_index_in_dim(split, 1 - core, 1, keepdims=False),
        )

    seg, mem, comp = seg_input[:, 0], memory[:, 0], compressed[:, 0]
    gy_own, comp_cot = out_grad[:, 0], comp_grad[:, 0]

    kept, sent = zip(*[halves(x) for x in (comp, mem, seg, gy_own)])
    came = swap(jnp.concatenate(sent, axis=1))
    kept = jnp.concatenate(kept, axis=1)
    pairs = by_core(kept, came, 1).reshape(2 * micros, -1, D)
    hc, hm, hs = comp_rows // 2, mem_rows // 2, seg_rows // 2
    source_rows = hc + hm + hs
    source = lax.all_to_all(
        pairs[:, :source_rows], "ffn", split_axis=0, concat_axis=0, tiled=True
    )
    gy_all = lax.all_gather(pairs[:, source_rows:], "ffn", axis=1, tiled=True)

    fills = jnp.concatenate([comp_fill, mem_fill], axis=1).astype(F32)
    twin_fills = swap(fills)
    pair_micro, pair_core = layer // 2, layer % 2
    counts = lax.dynamic_index_in_dim(
        jnp.where(pair_core == core, fills, twin_fills), pair_micro, 0, keepdims=False
    ).astype(jnp.int32)

    memory_pos = layer * mem_rows + jnp.arange(mem_rows, dtype=jnp.int32)
    alive = memory_pos[None, :] >= M - mem_fill
    flat = jnp.where(alive[:, :, None], mem, jnp.zeros_like(mem))
    flat = flat.reshape(micros * (mem_rows // 3), 3 * D)
    new_compressed = (matmul(flat, conv_weight) + conv_bias).astype(BF)
    new_compressed = new_compressed.reshape(micros, 1, mem_rows // 3, D)
    cot_rows = comp_cot.reshape(-1, D)
    conv_part = contract_rows(flat, cot_rows).astype(BF)
    conv_part = lax.psum_scatter(conv_part, "dp", scatter_dimension=0, tiled=True)
    conv_part = lax.psum_scatter(conv_part, "ffn", scatter_dimension=0, tiled=True)
    conv_grad = lax.all_gather(conv_part, ("dp", "ffn"), axis=0, tiled=True).astype(F32)
    conv_bias_part = jnp.sum(cot_rows.astype(F32), axis=0)
    down_bias_part = jnp.sum(gy_own.astype(F32), axis=(0, 1))

    source_f = source.reshape(layers * source_rows, D).astype(F32)
    source_hat, source_inverse = statistics(source_f)
    normed_half = (source_hat * attn_gain + attn_shift).astype(BF)
    normed_pair = by_core(normed_half, swap(normed_half), 0)
    normed_pair = normed_pair.reshape(2, layers, source_rows, D)
    sections = []
    start = 0
    for height in (hc, hm, hs):
        piece = normed_pair[:, :, start : start + height]
        sections.append(piece.transpose(1, 0, 2, 3).reshape(2 * layers * height, D))
        start += height
    normed = jnp.concatenate(sections, axis=0)
    own_columns = lax.dynamic_slice(attn_weights, (0, core * HALF), (4 * D, HALF))
    w_query, w_key, w_value = own_columns[:D], own_columns[D : 2 * D], own_columns[2 * D : 3 * D]
    w_out = attn_weights[3 * D :]
    w_out_rows = lax.dynamic_slice(attn_weights, (3 * D + core * HALF, 0), (HALF, D))
    normed_queries = normed[CM + M :]
    queries = matmul(normed_queries, w_query).astype(BF)
    keys = matmul(normed, w_key).astype(BF)
    values = matmul(normed, w_value).astype(BF)

    table = lax.dynamic_slice(rel_table, (core * OH, 0), (OH, NB))
    query_blocks = SEG // PW
    first_block = (CM + M) // PW
    extended = jnp.concatenate([jnp.full((OH, query_blocks - 1), MASKED, F32), table], axis=1)
    offset = first_block + query_blocks - 1
    bias = jnp.stack(
        [extended[:, offset - b : offset - b + query_blocks] for b in range(NB)], axis=1
    )
    bias = jnp.broadcast_to(bias[..., None], (OH, NB, query_blocks, PW)).reshape(OH, NB, SEG)
    mixed_own, attention = attention_forward(counts, queries, keys, values, bias)
    mixed = by_core(mixed_own, swap(mixed_own), 1).reshape(SEG, D)

    def own_rows(value):
        split = value.reshape(layers, 2, hs, D)
        return lax.dynamic_index_in_dim(split, core, 1, keepdims=False).reshape(layers * hs, D)

    segment_half = source.reshape(layers, source_rows, D)[:, hc + hm :]
    segment_half = segment_half.reshape(layers * hs, D).astype(F32)
    residual = segment_half + matmul(own_rows(mixed), w_out)
    residual_hat, residual_inverse = statistics(residual)
    ffn_in = (residual_hat * ffn_gain + ffn_shift).astype(BF)

    ffn_rows = lax.all_gather(ffn_in, "ffn", axis=0, tiled=True).reshape(layers, layers * hs, D)
    place = layer.reshape(1).astype(jnp.int32)
    parts, grad_parts, up_bias_part, weight_parts = feed_forward(
        place, ffn_rows, gy_all, w_up, b_up, w_down, residual + b_down, streams
    )
    weight_sum = lax.psum_scatter(weight_parts, "dp", scatter_dimension=0, tiled=True)[0]
    weight_sum = weight_sum.astype(F32)
    up_grad = weight_sum[0]
    down_grad = weight_sum[1].T
    layer_rows = lax.psum_scatter(parts, "ffn", scatter_dimension=1, tiled=True)
    grad_ffn_in = lax.psum_scatter(
        grad_parts.reshape(layers * layers * hs, D), "ffn", scatter_dimension=0, tiled=True
    ).astype(F32)

    def to_owners(value):
        split = value.reshape(micros, 2, hs, D)
        stay = lax.dynamic_index_in_dim(split, core, 1, keepdims=False)
        other = swap(lax.dynamic_index_in_dim(split, 1 - core, 1, keepdims=False))
        return by_core(stay, other, 1).reshape(micros, 1, 2 * hs, D)

    layer_out = to_owners(layer_rows)

    ffn_gain_part = jnp.sum(grad_ffn_in * residual_hat, axis=0)
    ffn_shift_part = jnp.sum(grad_ffn_in, axis=0)
    gy_half = lax.dynamic_index_in_dim(gy_all, layer, 0, keepdims=False).astype(F32)
    grad_residual = gy_half + norm_pull(residual_hat, residual_inverse, grad_ffn_in * ffn_gain)
    branch_half = grad_residual.astype(BF).reshape(layers, hs, D)
    grad_branch = by_core(branch_half, swap(branch_half), 1).reshape(SEG, D)

    grad_mixed = times_transposed(grad_branch, w_out_rows).astype(BF)
    branch_columns = lax.dynamic_slice(grad_branch, (0, core * HALF), (SEG, HALF))
    out_grad_part = contract_rows(mixed, branch_columns)
    grad_query, grad_key, grad_value, sums = attention_backward(
        attention, queries, keys, values, grad_mixed
    )
    query_part = contract_rows(normed_queries, grad_query)
    key_part = contract_rows(normed, grad_key)
    value_part = contract_rows(normed, grad_value)
    grad_normed = (
        times_transposed(grad_query, w_query)
        + times_transposed(grad_key[CM + M :], w_key)
        + times_transposed(grad_value[CM + M :], w_value)
    ).astype(BF)
    grad_normed = grad_normed.reshape(layers, 2, hs, D)
    grad_stay = lax.dynamic_index_in_dim(grad_normed, core, 1, keepdims=False).astype(F32)
    grad_came = swap(lax.dynamic_index_in_dim(grad_normed, 1 - core, 1, keepdims=False))
    grad_normed = (grad_stay + grad_came.astype(F32)).reshape(layers * hs, D)
    segment_hat = source_hat.reshape(layers, source_rows, D)[:, hc + hm :].reshape(-1, D)
    segment_inverse = source_inverse.reshape(layers, source_rows, 1)[:, hc + hm :].reshape(-1, 1)
    grad_segment = grad_residual + norm_pull(
        segment_hat, segment_inverse, grad_normed * attn_gain
    )
    grad_segment = lax.all_to_all(
        grad_segment.astype(BF).reshape(layers, hs, D),
        "ffn", split_axis=0, concat_axis=0, tiled=True,
    )
    seg_grad = to_owners(grad_segment).astype(F32)

    def column_sums(value):
        return jnp.sum(value.astype(F32), axis=0)

    shift_part = (
        jnp.sum(w_query.astype(F32) * column_sums(grad_query), axis=1)
        + jnp.sum(w_key.astype(F32) * column_sums(grad_key), axis=1)
        + jnp.sum(w_value.astype(F32) * column_sums(grad_value), axis=1)
    )
    product = (
        jnp.sum(w_query.astype(F32) * query_part, axis=1)
        + jnp.sum(w_key.astype(F32) * key_part, axis=1)
        + jnp.sum(w_value.astype(F32) * value_part, axis=1)
    )
    gain_part = (product - attn_shift * shift_part) / attn_gain

    stack = jnp.stack([query_part, key_part, value_part, out_grad_part]).astype(BF)
    bits = streams.bit_length() - 1
    piece_rows = 4 * D // (streams * layers)
    chunks = stack.reshape((2,) * (bits - 1) + (2, layers, piece_rows, HALF))

    def reduce_groups(value, order):
        left = list(range(bits - 1, 0, -1))
        for bit in order:
            axis = left.index(bit)
            mine = (stream >> bit) & 1
            stay = lax.dynamic_index_in_dim(value, mine, axis, keepdims=False)
            goes = lax.dynamic_index_in_dim(value, 1 - mine, axis, keepdims=False)
            other = lax.ppermute(goes, "dp", [(i, i ^ (1 << bit)) for i in range(streams)])
            value = (stay.astype(F32) + other.astype(F32)).astype(BF)
            left.pop(axis)
        return value

    order = list(range(1, bits))
    lead = (slice(None),) * (bits - 1)
    low = reduce_groups(chunks[lead + (0,)], order)
    high = reduce_groups(chunks[lead + (1,)], order[::-1])
    both = jnp.stack([low, high], axis=1)
    both = lax.psum_scatter(both, "ffn", scatter_dimension=0, tiled=True)[0]
    stay = lax.dynamic_index_in_dim(both, core, 0, keepdims=False)
    other = swap(lax.dynamic_index_in_dim(both, 1 - core, 0, keepdims=False))
    attn_weights_grad = by_core(stay, other, 1).reshape(piece_rows, D).astype(F32)

    tile_sums = jnp.sum(sums.reshape(OH, NB, query_blocks, PW), axis=-1)
    distance = (
        first_block
        + jnp.arange(query_blocks, dtype=jnp.int32)[None, :]
        - jnp.arange(NB, dtype=jnp.int32)[:, None]
    )
    one_hot = (distance[:, :, None] == jnp.arange(NB, dtype=jnp.int32)).astype(F32)
    table_part = jnp.einsum("hkq,kqn->hn", tile_sums, one_hot, precision=lax.Precision.HIGHEST)
    table_row = lax.dynamic_update_slice(jnp.zeros((H, NB), F32), table_part, (core * OH, 0))
    table_row = jnp.pad(table_row.reshape(-1), (0, D - H * NB))
    up_bias_rows = lax.dynamic_update_slice(
        jnp.zeros((layers, hidden_local), F32), up_bias_part, (layer, 0)
    ).reshape(-1, D)
    up_bias_count = up_bias_rows.shape[0]
    small = jnp.concatenate(
        [
            jnp.stack(
                [gain_part, shift_part, ffn_gain_part, ffn_shift_part, down_bias_part,
                 conv_bias_part, table_row]
            ),
            up_bias_rows,
        ]
    )
    for bit in range(bits):
        small = small + lax.ppermute(small, "dp", [(i, i ^ (1 << bit)) for i in range(streams)])
    for bit in range(layers.bit_length() - 1):
        small = small + lax.ppermute(small, "ffn", [(i, i ^ (1 << bit)) for i in range(layers)])
    return (
        layer_out,
        new_compressed,
        seg_grad,
        small[0],
        small[1],
        attn_weights_grad,
        small[6, : H * NB].reshape(H, NB),
        small[2],
        small[3],
        up_grad,
        small[7 : 7 + up_bias_count].reshape(-1),
        down_grad,
        small[4],
        conv_grad,
        small[5],
    )


def solution(mesh):
    return jax.shard_map(
        on_device,
        mesh=mesh,
        in_specs=(
            P(None, "dp", "ffn", None),
            P(None, "dp", "ffn", None),
            P(None, "dp", "ffn", None),
            P(None, "dp"),
            P(None, "dp"),
            P(),
            P(),
            P(),
            P(),
            P(),
            P(),
            P(None, "ffn"),
            P("ffn"),
            P("ffn", None),
            P(),
            P(),
            P(),
            P(None, "dp", "ffn", None),
            P(None, "dp", "ffn", None),
        ),
        out_specs=(
            P(None, "dp", "ffn", None),
            P(None, "dp", "ffn", None),
            P(None, "dp", "ffn", None),
            P(),
            P(),
            P(("dp", "ffn"), None),
            P(),
            P(),
            P(),
            P("dp", "ffn"),
            P(),
            P("ffn", "dp"),
            P(),
            P(),
            P(),
        ),
        check_vma=False,
    )
```

```python
import functools
import math

import jax
import jax.numpy as jnp
from jax import lax
from jax.experimental import pallas as pl
from jax.experimental.pallas import tpu as pltpu
from jax.sharding import PartitionSpec as P

D = 1024
H = 8
HD = 128
SEG = 512
M = 384
CM = 512
PW = 64
KR = 1408
NB = 22
OH = 4
HALF = OH * HD
EPSILON = 1e-05
MASKED = -1e30
SCALE = HD ** (-0.5)
BF = jnp.bfloat16
F32 = jnp.float32


def statistics(rows_in):
    centre = jnp.mean(rows_in, axis=-1, keepdims=True)
    centred = rows_in - centre
    variance = jnp.mean(centred * centred, axis=-1, keepdims=True)
    inverse = lax.rsqrt(variance + EPSILON)
    return centred * inverse, inverse


def matmul(left, right):
    return jnp.dot(left, right, preferred_element_type=F32)


def contract_rows(left, right):
    return lax.dot_general(left, right, (((0,), (0,)), ((), ())), preferred_element_type=F32)


def times_transposed(left, right):
    return lax.dot_general(left, right, (((1,), (1,)), ((), ())), preferred_element_type=F32)


def together(*values):
    return lax.optimization_barrier(values)


def norm_pull(xhat, inverse, scaled):
    mean_a = jnp.mean(scaled, axis=-1, keepdims=True)
    mean_b = jnp.mean(scaled * xhat, axis=-1, keepdims=True)
    return (scaled - mean_a - xhat * mean_b) * inverse


def norm_kernel(x_ref, gain_ref, shift_ref, _, out_ref):
    hat, _ = statistics(x_ref[0].astype(F32))
    out_ref[0] = (hat * gain_ref[...] + shift_ref[...]).astype(BF)


def norm_rows(rows, count, gain, shift, earlier):
    layers = rows.shape[0]
    return pl.pallas_call(
        norm_kernel,
        grid=(layers,),
        in_specs=[
            pl.BlockSpec((1, count, D), lambda i: (i, 0, 0)),
            pl.BlockSpec((1, D), lambda i: (0, 0)),
            pl.BlockSpec((1, D), lambda i: (0, 0)),
            pl.BlockSpec(memory_space=pl.ANY),
        ],
        out_specs=pl.BlockSpec((1, count, D), lambda i: (i, 0, 0)),
        out_shape=jax.ShapeDtypeStruct((layers, count, D), BF),
        cost_estimate=pl.CostEstimate(
            flops=8 * layers * count * D, bytes_accessed=4 * layers * count * D, transcendentals=0
        ),
        name="norm_rows",
    )(rows, gain.reshape(1, D), shift.reshape(1, D), earlier)


def attention_forward_kernel(counts, q_ref, k_ref, v_ref, bias_ref, o_ref, p_ref):
    comp_low = CM - counts[0]
    mem_low = CM + M - counts[1]
    for tile in range(SEG // HD):
        cols = slice(tile * HD, (tile + 1) * HD)
        seen = CM + M + (tile + 1) * HD
        raw = times_transposed(k_ref[:seen, :], q_ref[cols, :]) * SCALE
        blocks = seen // PW
        raw = (
            raw.reshape(blocks, PW, HD) + bias_ref[0, :blocks, cols].reshape(blocks, 1, HD)
        ).reshape(seen, HD)
        key_pos = lax.broadcasted_iota(jnp.int32, (seen, HD), 0)
        query_pos = CM + M + tile * HD + lax.broadcasted_iota(jnp.int32, (seen, HD), 1)
        low = jnp.where(key_pos < CM, comp_low, jnp.where(key_pos < CM + M, mem_low, 0))
        scores = jnp.where((key_pos >= low) & (key_pos <= query_pos), raw, MASKED)
        top = jnp.max(scores, axis=0, keepdims=True)
        expanded = jnp.exp(scores - top)
        total = jnp.sum(expanded, axis=0, keepdims=True)
        attention = (expanded * (1.0 / total)).astype(BF)
        p_ref[0, :seen, cols] = attention
        if seen < KR:
            p_ref[0, seen:, cols] = jnp.zeros((KR - seen, HD), BF)
        mixed = contract_rows(v_ref[:seen, :], attention)
        o_ref[cols, :] = mixed.T.astype(BF)


def attention_forward(counts, queries, keys, values, bias):
    return pl.pallas_call(
        attention_forward_kernel,
        grid=(OH,),
        in_specs=[
            pl.BlockSpec(memory_space=pltpu.SMEM),
            pl.BlockSpec((SEG, HD), lambda h: (0, h)),
            pl.BlockSpec((KR, HD), lambda h: (0, h)),
            pl.BlockSpec((KR, HD), lambda h: (0, h)),
            pl.BlockSpec((1, NB, SEG), lambda h: (h, 0, 0)),
        ],
        out_specs=[
            pl.BlockSpec((SEG, HD), lambda h: (0, h)),
            pl.BlockSpec((1, KR, SEG), lambda h: (h, 0, 0)),
        ],
        out_shape=[
            jax.ShapeDtypeStruct((SEG, HALF), BF),
            jax.ShapeDtypeStruct((OH, KR, SEG), BF),
        ],
        cost_estimate=pl.CostEstimate(
            flops=4 * OH * SEG * KR * HD, bytes_accessed=10 << 20, transcendentals=OH * SEG * KR
        ),
        name="attention_forward",
    )(counts, queries, keys, values, bias)


def half_rows(ref, half, rows):
    pieces = SEG // (2 * rows)
    return jnp.concatenate(
        [ref[pl.ds(pl.multiple_of((2 * i + half) * rows, rows), rows), :] for i in range(pieces)]
    )


def attention_backward_kernel(
    core, p_ref, q_ref, k_ref, v_ref, mine_ref, twin_ref, out_ref,
    dq_ref, dk_ref, dv_ref, columns_ref, sums_ref, ds_ref, g_ref, *, rows,
):
    weight = out_ref[...]
    for half, branch in ((core[0], mine_ref), (1 - core[0], twin_ref)):
        part = times_transposed(branch[...], weight).astype(BF)
        for i in range(SEG // (2 * rows)):
            start = pl.multiple_of((2 * i + half) * rows, rows)
            g_ref[pl.ds(start, rows), :] = part[i * rows : (i + 1) * rows]
    query_sum = jnp.zeros((1, HD), F32)
    block_sums = []
    for tile in range(SEG // HD):
        cols = slice(tile * HD, (tile + 1) * HD)
        seen = CM + M + (tile + 1) * HD
        blocks = seen // PW
        attention = p_ref[0, :seen, cols].astype(F32)
        grad_attention = times_transposed(v_ref[:seen, :], g_ref[cols, :])
        inner = jnp.sum(attention * grad_attention, axis=0, keepdims=True)
        grad_scores = (attention * (grad_attention - inner)).astype(BF)
        ds_ref[:seen, cols] = grad_scores
        block_sum = jnp.sum(grad_scores.astype(F32).reshape(blocks, PW, HD), axis=1)
        if seen < KR:
            ds_ref[seen:, cols] = jnp.zeros((KR - seen, HD), BF)
            block_sum = jnp.concatenate([block_sum, jnp.zeros((NB - blocks, HD), F32)], axis=0)
        block_sums.append(block_sum)
        grad_query = contract_rows(k_ref[:seen, :], grad_scores) * SCALE
        grad_query = grad_query.T.astype(BF)
        dq_ref[cols, :] = grad_query
        query_sum += jnp.sum(grad_query.astype(F32), axis=0, keepdims=True)
    grad_key = (matmul(ds_ref[...], q_ref[...]) * SCALE).astype(BF)
    dk_ref[...] = grad_key
    grad_value = matmul(p_ref[0], g_ref[...]).astype(BF)
    dv_ref[...] = grad_value
    columns_ref[...] = jnp.concatenate(
        [
            query_sum,
            jnp.sum(grad_key.astype(F32), axis=0, keepdims=True),
            jnp.sum(grad_value.astype(F32), axis=0, keepdims=True),
            jnp.zeros((1, HD), F32),
        ],
        axis=0,
    )
    picks = (
        lax.broadcasted_iota(jnp.int32, (SEG, HD), 0) // PW
        == lax.broadcasted_iota(jnp.int32, (SEG, HD), 1)
    ).astype(F32)
    sums_ref[0] = jnp.dot(
        jnp.concatenate(block_sums, axis=1), picks,
        precision=lax.Precision.HIGHEST, preferred_element_type=F32,
    )


def attention_backward(core, attention, queries, keys, values, mine, twin, attn_weights, rows):
    rows_of = lambda n: pl.BlockSpec((n, HD), lambda h, core: (0, h))
    whole = pl.BlockSpec((SEG // 2, D), lambda h, core: (0, 0))
    return pl.pallas_call(
        functools.partial(attention_backward_kernel, rows=rows),
        grid_spec=pltpu.PrefetchScalarGridSpec(
            num_scalar_prefetch=1,
            grid=(OH,),
            in_specs=[
                pl.BlockSpec((1, KR, SEG), lambda h, core: (h, 0, 0)),
                rows_of(SEG),
                rows_of(KR),
                rows_of(KR),
                whole,
                whole,
                pl.BlockSpec((HD, D), lambda h, core: (3 * H + OH * core[0] + h, 0)),
            ],
            out_specs=[
                rows_of(SEG),
                rows_of(KR),
                rows_of(KR),
                rows_of(4),
                pl.BlockSpec((1, NB, HD), lambda h, core: (h, 0, 0)),
            ],
            scratch_shapes=[pltpu.VMEM((KR, SEG), BF), pltpu.VMEM((SEG, HD), BF)],
        ),
        out_shape=[
            jax.ShapeDtypeStruct((SEG, HALF), BF),
            jax.ShapeDtypeStruct((KR, HALF), BF),
            jax.ShapeDtypeStruct((KR, HALF), BF),
            jax.ShapeDtypeStruct((4, HALF), F32),
            jax.ShapeDtypeStruct((OH, NB, HD), F32),
        ],
        cost_estimate=pl.CostEstimate(
            flops=8 * OH * SEG * KR * HD, bytes_accessed=14 << 20, transcendentals=0
        ),
        name="attention_backward",
    )(core, attention, queries, keys, values, mine, twin, attn_weights)


def residual_kernel(
    core, mine_ref, twin_ref, out_ref, seg_ref, gain_ref, shift_ref, residual_ref, in_ref, *, rows
):
    half = core[0]
    total = seg_ref[...].astype(F32)
    for which, ref in ((half, mine_ref), (1 - half, twin_ref)):
        weight = out_ref[pl.ds(pl.multiple_of(which * HALF, HALF), HALF), :]
        total += matmul(half_rows(ref, half, rows), weight)
    residual_ref[...] = total
    hat, _ = statistics(total)
    in_ref[...] = (hat * gain_ref[...] + shift_ref[...]).astype(BF)


def residual_norm(core, mine, twin, attn_weights, segment, gain, shift, rows):
    count = SEG // 2
    whole = lambda a, b: pl.BlockSpec((a, b), lambda i, core: (0, 0))
    return pl.pallas_call(
        functools.partial(residual_kernel, rows=rows),
        grid_spec=pltpu.PrefetchScalarGridSpec(
            num_scalar_prefetch=1,
            grid=(1,),
            in_specs=[
                whole(SEG, HALF),
                whole(SEG, HALF),
                pl.BlockSpec((D, D), lambda i, core: (3, 0)),
                whole(count, D),
                whole(1, D),
                whole(1, D),
            ],
            out_specs=[whole(count, D), whole(count, D)],
        ),
        out_shape=[
            jax.ShapeDtypeStruct((count, D), F32),
            jax.ShapeDtypeStruct((count, D), BF),
        ],
        cost_estimate=pl.CostEstimate(
            flops=2 * count * D * D, bytes_accessed=6 << 20, transcendentals=0
        ),
        name="residual_norm",
    )(core, mine, twin, attn_weights, segment, gain.reshape(1, D), shift.reshape(1, D))


def norm_backward_kernel(
    residual_ref, own_ref, came_ref, gy_ref, gain_ref, grad_ref, branch_ref, sums_ref
):
    hat, inverse = statistics(residual_ref[...])
    grad = own_ref[...] + came_ref[...].astype(F32)
    sums_ref[...] = jnp.concatenate(
        [jnp.sum(grad * hat, axis=0, keepdims=True), jnp.sum(grad, axis=0, keepdims=True)], axis=0
    )
    total = gy_ref[...].astype(F32) + norm_pull(hat, inverse, grad * gain_ref[...])
    grad_ref[...] = total
    branch_ref[...] = total.astype(BF)


def norm_backward(residual, own, came, gy, gain):
    count = residual.shape[0]
    return pl.pallas_call(
        norm_backward_kernel,
        out_shape=[
            jax.ShapeDtypeStruct((count, D), F32),
            jax.ShapeDtypeStruct((count, D), BF),
            jax.ShapeDtypeStruct((2, D), F32),
        ],
        cost_estimate=pl.CostEstimate(
            flops=20 * count * D, bytes_accessed=6 << 20, transcendentals=0
        ),
        name="norm_backward",
    )(residual, own, came, gy, gain.reshape(1, D))


def owners_kernel(
    seg_ref, keep_ref, came_ref, grad_ref, gain_ref, residual_ref, part_ref, next_ref, bias_ref,
    out_ref,
):
    layers, _, rows, _ = out_ref.shape
    result = residual_ref[...] + (part_ref[...] + next_ref[...].astype(F32) + bias_ref[...])
    out_ref[:, 0] = result.astype(BF).reshape(layers, rows, D)
    hat, inverse = statistics(seg_ref[...].astype(F32))
    cotangent = (keep_ref[...] + came_ref[...].astype(F32)) * gain_ref[...]
    result = grad_ref[...] + norm_pull(hat, inverse, cotangent)
    out_ref[:, 1] = result.astype(BF).reshape(layers, rows, D)


def owners_rows(segment, keep, came, grad, gain, residual, part, part_next, bias, layers):
    count = segment.shape[0]
    return pl.pallas_call(
        owners_kernel,
        out_shape=jax.ShapeDtypeStruct((layers, 2, count // layers, D), BF),
        cost_estimate=pl.CostEstimate(
            flops=20 * count * D, bytes_accessed=8 << 20, transcendentals=0
        ),
        name="owners_rows",
    )(
        segment, keep, came, grad, gain.reshape(1, D), residual, part, part_next,
        bias.reshape(1, D),
    )


def normed_kernel(
    core, dq_ref, dk_ref, dv_ref, wq_ref, wk_ref, wv_ref, keep_ref, send_ref, all_ref, *, rows
):
    total = times_transposed(dq_ref[...], wq_ref[...])
    total += times_transposed(dk_ref[CM + M :, :], wk_ref[...])
    total += times_transposed(dv_ref[CM + M :, :], wv_ref[...])
    all_ref[...] = total
    send_ref[...] = half_rows(all_ref, 1 - core[0], rows).astype(BF)
    keep_ref[...] = half_rows(all_ref, core[0], rows)


def normed_gradient(core, dq, dk, dv, weights, rows):
    width = D // 4
    whole = lambda n: pl.BlockSpec((n, HALF), lambda i, core: (0, 0))
    block = lambda m: pl.BlockSpec((width, HALF), lambda i, core: (i + 4 * m, 0))
    out = pl.BlockSpec((SEG // 2, width), lambda i, core: (0, i))
    return pl.pallas_call(
        functools.partial(normed_kernel, rows=rows),
        grid_spec=pltpu.PrefetchScalarGridSpec(
            num_scalar_prefetch=1,
            grid=(4,),
            in_specs=[whole(SEG), whole(KR), whole(KR), block(0), block(1), block(2)],
            out_specs=[out, out],
            scratch_shapes=[pltpu.VMEM((SEG, width), F32)],
        ),
        out_shape=[
            jax.ShapeDtypeStruct((SEG // 2, D), F32),
            jax.ShapeDtypeStruct((SEG // 2, D), BF),
        ],
        cost_estimate=pl.CostEstimate(
            flops=6 * SEG * D * HALF, bytes_accessed=8 << 20, transcendentals=0
        ),
        name="normed_gradient",
    )(core, dq, dk, dv, weights, weights, weights)


def feed_forward_kernel(packed, added, *refs):
    x_ref, gy_ref = refs[:2]
    if packed:
        bias_ref, weights_ref = refs[2:4]
        rest = refs[4:]
        pieces, _, height, hidden = weights_ref.shape
        up = weights_ref[:, 0].reshape(pieces * height, hidden)
        down = weights_ref[:, 1].reshape(pieces * height, hidden)
    else:
        bias_ref, up_ref, down_ref = refs[2:5]
        rest = refs[5:]
        up, down = up_ref[...], down_ref[...]
    if added:
        prev_part, prev_grad = rest[:2]
        rest = rest[2:]
    part_ref, grad_ref, act_ref, pre_ref, sum_ref = rest
    rows = x_ref[...]
    hidden = matmul(rows, up) + bias_ref[...]
    normal = 0.5 * (1.0 + lax.erf(hidden * math.sqrt(0.5)))
    slope = normal + hidden * jnp.exp(-0.5 * hidden * hidden) * (1.0 / math.sqrt(2.0 * math.pi))
    activated = (hidden * normal).astype(BF)
    act_ref[...] = activated
    grad_hidden = times_transposed(gy_ref[...], down)
    grad_pre = (grad_hidden * slope).astype(BF)
    pre_ref[...] = grad_pre
    grad = times_transposed(grad_pre, up)
    part = matmul(activated, down)
    if added:
        grad = grad + prev_grad[...]
        part = part + prev_part[...]
    grad_ref[...] = grad.astype(grad_ref.dtype)
    part_ref[...] = part.astype(part_ref.dtype)
    sum_ref[...] = jnp.sum(grad_pre.astype(F32), axis=0, keepdims=True)


def feed_forward(rows, gy, bias, weights, previous, dtype):
    height = rows.shape[0]
    hidden = bias.shape[-1]
    packed = len(weights) == 1
    operands = [rows, gy, bias, *weights, *previous]
    return pl.pallas_call(
        functools.partial(feed_forward_kernel, packed, bool(previous)),
        out_shape=[
            jax.ShapeDtypeStruct((height, D), dtype),
            jax.ShapeDtypeStruct((height, D), dtype),
            jax.ShapeDtypeStruct((height, hidden), BF),
            jax.ShapeDtypeStruct((height, hidden), BF),
            jax.ShapeDtypeStruct((1, hidden), F32),
        ],
        compiler_params=pltpu.CompilerParams(vmem_limit_bytes=60 << 20),
        cost_estimate=pl.CostEstimate(
            flops=32 * height * D * hidden,
            bytes_accessed=32 << 20,
            transcendentals=8 * height * hidden,
        ),
        name="feed_forward",
    )(*operands)


def weight_products(ins, shards=2):
    left = [(ins[0], ins[1]), (ins[2], ins[3])]
    for shard in range(shards):
        right = ins[4 + 4 * shard : 8 + 4 * shard]
        for which in range(2):
            total = contract_rows(left[which][0][...], right[2 * which][...])
            total += contract_rows(left[which][1][...], right[2 * which + 1][...])
            yield shard, which, total


def weight_send_kernel(place, *refs):
    *ins, send_ref = refs
    for shard, which, total in weight_products(ins):
        send_ref[0, shard, which] = total.astype(BF)


def weight_keep_kernel(place, *refs):
    *ins, came_ref, near_keep, near_send, far_keep, far_send = refs
    step = pl.program_id(0)
    high, low = step // 2, step % 2
    for shard, which, total in weight_products(ins):
        total = (total + came_ref[0, shard, which].astype(F32)).astype(BF)
        bit, other, mine = ((high, low, place[1]), (low, high, place[2]))[shard]
        keep, send = ((near_keep, near_send), (far_keep, far_send))[shard]

        @pl.when(bit == mine)
        def _():
            keep[other, which] = total

        @pl.when(bit != mine)
        def _():
            send[other, which] = total


def weight_gradients(place, left, right, width, came=None):
    count, hidden = right[0].shape
    steps = D // width // 2
    send = came is None

    def piece(i, place):
        return 0, 2 * i + (1 - place[0] if send else place[0])

    each = pl.BlockSpec((1, 2, 2, width, hidden), lambda i, place: (i, 0, 0, 0, 0))
    quarter = pl.BlockSpec((2, 2, width, hidden), lambda i, place: (0, 0, 0, 0))
    quarter_shape = jax.ShapeDtypeStruct((2, 2, width, hidden), BF)
    return pl.pallas_call(
        weight_send_kernel if send else weight_keep_kernel,
        grid_spec=pltpu.PrefetchScalarGridSpec(
            num_scalar_prefetch=1,
            grid=(steps,),
            in_specs=[pl.BlockSpec((count, width), piece)] * 4
            + [pl.BlockSpec((count, hidden), lambda i, place: (0, 0))] * 8
            + ([] if send else [each]),
            out_specs=each if send else [quarter] * 4,
        ),
        out_shape=jax.ShapeDtypeStruct((steps, 2, 2, width, hidden), BF)
        if send
        else [quarter_shape] * 4,
        cost_estimate=pl.CostEstimate(
            flops=16 * count * D * hidden, bytes_accessed=16 << 20, transcendentals=0
        ),
        name="weight_send" if send else "weight_keep",
    )(place, *left, *right, *(() if send else (came,)))


def projection_kernel(
    place, core, normed_ref, mixed_mine, mixed_twin, dq_ref, dk_ref, dv_ref,
    branch_mine, branch_twin, wq_ref, wk_ref, wv_ref, columns_ref,
    low_keep, low_send, high_keep, high_send, vector_ref, mixed_ref, *, rows,
):
    step = pl.program_id(0)
    half_steps = pl.num_programs(0) // 2
    half = core[0]
    gain = jnp.zeros((HD, HD), F32)
    shift = jnp.zeros((HD, HD), F32)
    totals = []
    for which, (start, right, weight_ref) in enumerate(
        ((CM + M, dq_ref, wq_ref), (0, dk_ref, wk_ref), (0, dv_ref, wv_ref))
    ):
        total = contract_rows(normed_ref[start:, :], right[...])
        totals.append(total.astype(BF))
        weight = weight_ref[...].astype(F32)
        sums = columns_ref[which : which + 1, :]
        for part in range(OH):
            span = slice(part * HD, (part + 1) * HD)
            gain += weight[:, span] * total[:, span]
            shift += weight[:, span] * sums[:, span]
    mixed_ref[...] = jnp.where(
        step // half_steps == half, mixed_mine[...].astype(F32), mixed_twin[...].astype(F32)
    )
    total = contract_rows(half_rows(mixed_ref, half, rows).astype(BF), branch_mine[...])
    total += contract_rows(half_rows(mixed_ref, 1 - half, rows).astype(BF), branch_twin[...])
    totals.append(total.astype(BF))
    vector_ref[0:1, :] = jnp.sum(gain.T, axis=0, keepdims=True)
    vector_ref[1:2, :] = jnp.sum(shift.T, axis=0, keepdims=True)
    vector_ref[2:, :] = jnp.zeros((6, HD), F32)

    def store(keep, send, by_high):
        for which, total in enumerate(totals):
            high, low = which // 2, which % 2
            bit, other, mine = (high, low, place[1]) if by_high else (low, high, place[2])

            @pl.when(bit == mine)
            def _():
                keep[other, 0] = total

            @pl.when(bit != mine)
            def _():
                send[other, 0] = total

    @pl.when(step < half_steps)
    def _():
        store(low_keep, low_send, False)

    @pl.when(step >= half_steps)
    def _():
        store(high_keep, high_send, True)


def projection_gradients(
    place, core, normed, mixed_mine, mixed_twin, dq, dk, dv, branch_mine, branch_twin,
    weights, columns, rows,
):
    steps = D // HD
    half = steps // 2
    whole = lambda n: pl.BlockSpec((n, HALF), lambda i, *_: (0, 0))
    head = pl.BlockSpec((SEG, HD), lambda i, *_: (0, i % OH))
    branch = pl.BlockSpec((SEG // 2, HALF), lambda i, place, core: (0, core[0]))
    weight = lambda m: pl.BlockSpec((HD, HALF), lambda i, *_: (i + m * steps, 0))
    first = pl.BlockSpec((2, 1, HD, HALF), lambda i, *_: (0, jnp.minimum(i, half - 1), 0, 0))
    last = pl.BlockSpec((2, 1, HD, HALF), lambda i, *_: (0, jnp.maximum(i - half, 0), 0, 0))
    shape = jax.ShapeDtypeStruct((2, half, HD, HALF), BF)
    return pl.pallas_call(
        functools.partial(projection_kernel, rows=rows),
        grid_spec=pltpu.PrefetchScalarGridSpec(
            num_scalar_prefetch=2,
            grid=(steps,),
            in_specs=[
                pl.BlockSpec((KR, HD), lambda i, *_: (0, i)),
                head, head,
                whole(SEG), whole(KR), whole(KR),
                branch, branch,
                weight(0), weight(1), weight(2),
                whole(4),
            ],
            out_specs=[first, first, last, last, pl.BlockSpec((8, HD), lambda i, *_: (0, i))],
            scratch_shapes=[pltpu.VMEM((SEG, HD), F32)],
        ),
        out_shape=[shape] * 4 + [jax.ShapeDtypeStruct((8, D), F32)],
        cost_estimate=pl.CostEstimate(
            flops=4 * (KR + SEG) * D * HALF, bytes_accessed=16 << 20, transcendentals=0
        ),
        name="projection_gradients",
    )(
        place, core, normed, mixed_mine, mixed_twin, dq, dk, dv, branch_mine, branch_twin,
        weights, weights, weights, columns,
    )


def on_device(
    seg_input,
    memory,
    compressed,
    mem_fill,
    comp_fill,
    attn_gain,
    attn_shift,
    attn_weights,
    rel_table,
    ffn_gain,
    ffn_shift,
    w_up,
    b_up,
    w_down,
    b_down,
    conv_weight,
    conv_bias,
    out_grad,
    comp_grad,
):
    streams = lax.axis_size("dp")
    layers = lax.axis_size("ffn")
    stream = lax.axis_index("dp")
    layer = lax.axis_index("ffn")
    core = stream % 2
    micros = seg_input.shape[0]
    seg_rows, mem_rows, comp_rows = seg_input.shape[2], memory.shape[2], compressed.shape[2]
    hidden_local = w_up.shape[1]
    twins = [(i, i ^ 1) for i in range(streams)]
    first = core == 0
    which_core = core.reshape(1).astype(jnp.int32)

    def swap(value):
        return lax.ppermute(value, "dp", twins)

    def by_core(mine, other, axis):
        return jnp.where(
            first, jnp.stack([mine, other], axis=axis), jnp.stack([other, mine], axis=axis)
        )

    def halves(value):
        split = value.reshape(micros, 2, value.shape[1] // 2, D)
        return (
            lax.dynamic_index_in_dim(split, core, 1, keepdims=False),
            lax.dynamic_index_in_dim(split, 1 - core, 1, keepdims=False),
        )

    seg, mem, comp = seg_input[:, 0], memory[:, 0], compressed[:, 0]
    gy_own, comp_cot = out_grad[:, 0], comp_grad[:, 0]

    kept, sent = zip(*[halves(x) for x in (comp, mem, seg, gy_own)])
    came = swap(jnp.concatenate(sent, axis=1))
    kept = jnp.concatenate(kept, axis=1)
    pairs = by_core(kept, came, 1).reshape(2 * micros, -1, D)
    hc, hm, hs = comp_rows // 2, mem_rows // 2, seg_rows // 2
    pairs, mem, comp_cot, b_up, comp_fill, gy_own = together(
        pairs, mem, comp_cot, b_up, comp_fill, gy_own
    )
    source_rows = hc + hm + hs
    source = lax.all_to_all(pairs, "ffn", split_axis=0, concat_axis=0, tiled=True)

    fills = jnp.concatenate([comp_fill, mem_fill], axis=1).astype(F32)
    twin_fills = swap(fills)
    pair_micro, pair_core = layer // 2, layer % 2
    counts = lax.dynamic_index_in_dim(
        jnp.where(pair_core == core, fills, twin_fills), pair_micro, 0, keepdims=False
    ).astype(jnp.int32)

    memory_pos = layer * mem_rows + jnp.arange(mem_rows, dtype=jnp.int32)
    alive = memory_pos[None, :] >= M - mem_fill
    flat = jnp.where(alive[:, :, None], mem, jnp.zeros_like(mem))
    flat = flat.reshape(micros * (mem_rows // 3), 3 * D)
    new_compressed = (matmul(flat, conv_weight) + conv_bias).astype(BF)
    new_compressed = new_compressed.reshape(micros, 1, mem_rows // 3, D)
    cot_rows = comp_cot.reshape(-1, D)
    conv_part = contract_rows(flat, cot_rows).astype(BF)
    conv_rows = lax.psum_scatter(conv_part, "dp", scatter_dimension=0, tiled=True)
    conv_bias_part = jnp.sum(cot_rows.astype(F32), axis=0)
    down_bias_part = jnp.sum(gy_own.astype(F32), axis=(0, 1))

    own_columns = lax.dynamic_slice(attn_weights, (0, core * HALF), (3 * D, HALF))
    table = lax.dynamic_slice(rel_table, (core * OH, 0), (OH, NB))
    query_blocks = SEG // PW
    first_block = (CM + M) // PW
    extended = jnp.concatenate([jnp.full((OH, query_blocks - 1), MASKED, F32), table], axis=1)
    offset = first_block + query_blocks - 1
    bias = jnp.stack(
        [extended[:, offset - b : offset - b + query_blocks] for b in range(NB)], axis=1
    )
    bias = jnp.broadcast_to(bias[..., None], (OH, NB, query_blocks, PW)).reshape(OH, NB, SEG)

    height = D // streams
    across = [(i, i ^ 2) for i in range(layers)]
    beside = [(i, i ^ 1) for i in range(layers)]
    carried = jnp.stack(
        [lax.dynamic_slice(w, (stream * height, 0), (height, hidden_local)) for w in (w_up, w_down)]
    )
    far_bias = lax.ppermute(b_up.reshape(1, hidden_local), "ffn", across)

    (
        source, new_compressed, carried, counts, bias, far_bias, own_columns,
        conv_bias_part, down_bias_part,
    ) = together(
        source, new_compressed, carried, counts, bias, far_bias, own_columns,
        conv_bias_part, down_bias_part,
    )
    w_query, w_key, w_value = own_columns[:D], own_columns[D : 2 * D], own_columns[2 * D :]
    gy_half = source[:, source_rows:].reshape(layers * hs, D)
    gy_next = lax.ppermute(gy_half, "ffn", beside)
    carried = lax.ppermute(carried, "ffn", across)

    normed_half = norm_rows(source, source_rows, attn_gain, attn_shift, conv_part)
    normed_pair = by_core(normed_half, swap(normed_half), 0)
    normed_pair = normed_pair.reshape(2, layers, source_rows, D)
    sections = []
    start = 0
    for count in (hc, hm, hs):
        piece = normed_pair[:, :, start : start + count]
        sections.append(piece.transpose(1, 0, 2, 3).reshape(2 * layers * count, D))
        start += count
    (normed,) = together(jnp.concatenate(sections, axis=0))
    queries = matmul(normed[CM + M :], w_query).astype(BF)
    keys = matmul(normed, w_key).astype(BF)
    values = matmul(normed, w_value).astype(BF)

    mixed_own, attention = attention_forward(counts, queries, keys, values, bias)
    mixed_own, carried, gy_next, conv_rows = together(mixed_own, carried, gy_next, conv_rows)
    far_weights = lax.all_gather(carried[None], "dp", axis=0, tiled=True)
    mixed_twin = swap(mixed_own)
    segment = source[:, hc + hm : source_rows].reshape(layers * hs, D)
    residual, ffn_in = residual_norm(
        which_core, mixed_own, mixed_twin, attn_weights, segment, ffn_gain, ffn_shift, hs
    )

    bits = streams.bit_length() - 1
    inner = bits - 3

    def partners(bit):
        return [(i, i ^ (1 << bit)) for i in range(streams)]

    def combine(stay, goes, bit):
        other = lax.ppermute(goes, "dp", partners(bit))
        return (stay.astype(F32) + other.astype(F32)).astype(BF)

    def reduce_over(value, axes, order):
        axes = list(axes)
        for bit in order:
            axis = axes.index(bit)
            mine = (stream >> bit) & 1
            stay = lax.dynamic_index_in_dim(value, mine, axis, keepdims=False)
            goes = lax.dynamic_index_in_dim(value, 1 - mine, axis, keepdims=False)
            value = combine(stay, goes, bit)
            axes.pop(axis)
        return value

    bias_row = b_up.reshape(1, hidden_local)
    ffn_next = lax.ppermute(ffn_in, "ffn", beside)
    near = (w_up, w_down)
    far = (far_weights,)
    own_part, own_grad, act_own, pre_own, sum_a = feed_forward(
        ffn_in, gy_half, bias_row, near, (), F32
    )
    next_part, next_grad, act_next, pre_next, sum_b = feed_forward(
        ffn_next, gy_next, bias_row, near, (), F32
    )
    next_part, next_grad, far_act_next, far_pre_next, sum_c = feed_forward(
        ffn_next, gy_next, far_bias, far, (next_part, next_grad), BF
    )
    grad_came = lax.ppermute(next_grad, "ffn", beside)
    part_came = lax.ppermute(next_part, "ffn", beside)
    own_part, own_grad, far_act_own, far_pre_own, sum_d = feed_forward(
        ffn_in, gy_half, far_bias, far, (own_part, own_grad), F32
    )
    grad_came, conv_rows = together(grad_came, conv_rows)
    conv_rows = lax.psum_scatter(conv_rows, "ffn", scatter_dimension=0, tiled=True)
    up_bias_part = sum_a + sum_b
    far_bias_part = sum_c + sum_d

    grad_residual, branch, norm_sums = norm_backward(
        residual, own_grad, grad_came, gy_half, ffn_gain
    )
    branch, far_pre_own = together(branch, far_pre_own)
    branch_twin = swap(branch)
    top, next_top = bits - 1, bits - 2
    lower = list(range(inner - 1, -1, -1))
    place = jnp.stack([(stream >> bit) & 1 for bit in (inner, top, next_top)]).astype(jnp.int32)
    factors = (
        (ffn_in, ffn_next, gy_half, gy_next),
        (pre_own, pre_next, act_own, act_next,
         far_pre_own, far_pre_next, far_act_own, far_act_next),
    )
    weight_came = lax.ppermute(
        weight_gradients(place, *factors, HD), "dp", partners(inner)
    )

    grad_query, grad_key, grad_value, columns, sums = attention_backward(
        which_core, attention, queries, keys, values, branch, branch_twin, attn_weights, hs
    )
    grad_query, conv_rows, part_came, weight_came = together(
        grad_query, conv_rows, part_came, weight_came
    )
    conv_grad = lax.all_gather(conv_rows, ("dp", "ffn"), axis=0, tiled=True).astype(F32)
    near_keep, near_send, far_keep, far_send = weight_gradients(place, *factors, HD, weight_came)
    grad_key, near_send, far_send = together(grad_key, near_send, far_send)
    normed_keep, normed_send = normed_gradient(
        which_core, grad_query, grad_key, grad_value, own_columns, hs
    )
    normed_came = swap(normed_send)
    low_keep, low_send, high_keep, high_send, vectors = projection_gradients(
        place, which_core, normed, mixed_own, mixed_twin, grad_query, grad_key, grad_value,
        branch, branch_twin, own_columns, columns, hs,
    )
    shift_part = vectors[1]
    gain_part = (vectors[0] - attn_shift * shift_part) / attn_gain

    rows_out = owners_rows(
        segment, normed_keep, normed_came, grad_residual, attn_gain, residual, own_part,
        part_came, b_down, layers,
    )
    rows_out = lax.all_to_all(rows_out, "ffn", split_axis=0, concat_axis=0, tiled=True)
    rows_out = rows_out.reshape(micros, 2, 2, hs, D)
    rows_stay = lax.dynamic_index_in_dim(rows_out, core, 1, keepdims=False)
    rows_came = swap(lax.dynamic_index_in_dim(rows_out, 1 - core, 1, keepdims=False))
    rows_out = by_core(rows_stay, rows_came, 2).reshape(micros, 2, 2 * hs, D)
    layer_out = rows_out[:, :1]
    seg_grad = rows_out[:, 1:].astype(F32)

    split = (2, 2) + (2,) * inner + (height, hidden_local)
    far_sum = combine(far_keep, far_send, next_top).reshape(split)
    far_sum = reduce_over(far_sum, [top, None] + lower, [top] + lower)
    near_sum = combine(near_keep, near_send, top).reshape(split)
    near_sum = reduce_over(near_sum, [next_top, None] + lower, [next_top] + lower)
    weight_sum = near_sum.astype(F32) + lax.ppermute(far_sum, "ffn", across).astype(F32)
    up_grad = weight_sum[0]
    down_grad = weight_sum[1].T

    piece_rows = 4 * D // (streams * layers)
    split = (2,) + (2,) * inner + (layers, piece_rows, HALF)
    rest = [bit for bit in lower if bit > 0]
    low = combine(low_keep, low_send, next_top).reshape(split)
    low = reduce_over(low, [top] + lower, [top] + rest)
    high = combine(high_keep, high_send, top).reshape(split)
    high = reduce_over(high, [next_top] + lower, [next_top] + rest)
    both = jnp.stack([low, high])
    if inner:
        both = reduce_over(both, [inner], [inner])
    both = lax.all_to_all(both, "ffn", split_axis=1, concat_axis=1, tiled=True)
    both, conv_grad = together(both, conv_grad)
    both = jnp.sum(both.astype(F32), axis=1).astype(BF)
    stay = lax.dynamic_index_in_dim(both, core, 0, keepdims=False)
    other = swap(lax.dynamic_index_in_dim(both, 1 - core, 0, keepdims=False))
    attn_weights_grad = by_core(stay, other, 1).reshape(piece_rows, D).astype(F32)

    tile_sums = sums[:, :, :query_blocks]
    distance = (
        first_block
        + jnp.arange(query_blocks, dtype=jnp.int32)[None, :]
        - jnp.arange(NB, dtype=jnp.int32)[:, None]
    )
    one_hot = (distance[:, :, None] == jnp.arange(NB, dtype=jnp.int32)).astype(F32)
    table_part = jnp.einsum("hkq,kqn->hn", tile_sums, one_hot, precision=lax.Precision.HIGHEST)
    table_row = lax.dynamic_update_slice(jnp.zeros((H, NB), F32), table_part, (core * OH, 0))
    table_row = jnp.pad(table_row.reshape(-1), (0, D - H * NB))
    up_bias_rows = lax.dynamic_update_slice(
        jnp.zeros((layers, hidden_local), F32), up_bias_part, (layer, 0)
    )
    up_bias_rows = lax.dynamic_update_slice(up_bias_rows, far_bias_part, (layer ^ 2, 0))
    up_bias_rows = up_bias_rows.reshape(-1, D)
    up_bias_count = up_bias_rows.shape[0]
    small = jnp.concatenate(
        [
            jnp.stack(
                [gain_part, shift_part, norm_sums[0], norm_sums[1], down_bias_part,
                 conv_bias_part, table_row]
            ),
            up_bias_rows,
        ]
    )
    small, seg_grad = together(small, seg_grad)
    for bit in range(bits):
        small = small + lax.ppermute(small, "dp", [(i, i ^ (1 << bit)) for i in range(streams)])
    for bit in range(layers.bit_length() - 1):
        small = small + lax.ppermute(small, "ffn", [(i, i ^ (1 << bit)) for i in range(layers)])
    return (
        layer_out,
        new_compressed,
        seg_grad,
        small[0],
        small[1],
        attn_weights_grad,
        small[6, : H * NB].reshape(H, NB),
        small[2],
        small[3],
        up_grad,
        small[7 : 7 + up_bias_count].reshape(-1),
        down_grad,
        small[4],
        conv_grad,
        small[5],
    )


def solution(mesh):
    return jax.shard_map(
        on_device,
        mesh=mesh,
        in_specs=(
            P(None, "dp", "ffn", None),
            P(None, "dp", "ffn", None),
            P(None, "dp", "ffn", None),
            P(None, "dp"),
            P(None, "dp"),
            P(),
            P(),
            P(),
            P(),
            P(),
            P(),
            P(None, "ffn"),
            P("ffn"),
            P("ffn", None),
            P(),
            P(),
            P(),
            P(None, "dp", "ffn", None),
            P(None, "dp", "ffn", None),
        ),
        out_specs=(
            P(None, "dp", "ffn", None),
            P(None, "dp", "ffn", None),
            P(None, "dp", "ffn", None),
            P(),
            P(),
            P(("dp", "ffn"), None),
            P(),
            P(),
            P(),
            P("dp", "ffn"),
            P(),
            P("ffn", "dp"),
            P(),
            P(),
            P(),
        ),
        check_vma=False,
    )
```

```python
import functools
import math

import jax
import jax.numpy as jnp
from jax import lax
from jax.experimental import pallas as pl
from jax.experimental.pallas import tpu as pltpu
from jax.sharding import PartitionSpec as P

D = 1024
H = 8
HD = 128
SEG = 512
M = 384
CM = 512
PW = 64
KR = 1408
NB = 22
OH = 4
TQ = 128
HALF = OH * HD
EPSILON = 1e-05
MASKED = -1e30
SCALE = HD ** (-0.5)
BF = jnp.bfloat16
F32 = jnp.float32


def statistics(rows_in):
    centre = jnp.mean(rows_in, axis=-1, keepdims=True)
    centred = rows_in - centre
    variance = jnp.mean(centred * centred, axis=-1, keepdims=True)
    inverse = lax.rsqrt(variance + EPSILON)
    return centred * inverse, inverse


def matmul(left, right):
    return jnp.dot(left, right, preferred_element_type=F32)


def contract_rows(left, right):
    return lax.dot_general(left, right, (((0,), (0,)), ((), ())), preferred_element_type=F32)


def times_transposed(left, right):
    return lax.dot_general(left, right, (((1,), (1,)), ((), ())), preferred_element_type=F32)


def together(*values):
    return lax.optimization_barrier(values)


def norm_pull(xhat, inverse, scaled):
    mean_a = jnp.mean(scaled, axis=-1, keepdims=True)
    mean_b = jnp.mean(scaled * xhat, axis=-1, keepdims=True)
    return (scaled - mean_a - xhat * mean_b) * inverse


def norm_kernel(x_ref, gain_ref, shift_ref, _, out_ref):
    hat, _ = statistics(x_ref[0].astype(F32))
    out_ref[0] = (hat * gain_ref[...] + shift_ref[...]).astype(BF)


def norm_rows(rows, count, gain, shift, earlier):
    layers = rows.shape[0]
    return pl.pallas_call(
        norm_kernel,
        grid=(layers,),
        in_specs=[
            pl.BlockSpec((1, count, D), lambda i: (i, 0, 0)),
            pl.BlockSpec((1, D), lambda i: (0, 0)),
            pl.BlockSpec((1, D), lambda i: (0, 0)),
            pl.BlockSpec(memory_space=pl.ANY),
        ],
        out_specs=pl.BlockSpec((1, count, D), lambda i: (i, 0, 0)),
        out_shape=jax.ShapeDtypeStruct((layers, count, D), BF),
        cost_estimate=pl.CostEstimate(flops=1 << 20, bytes_accessed=1 << 16, transcendentals=0),
        name="norm_rows",
    )(rows, gain.reshape(1, D), shift.reshape(1, D), earlier)


def attention_forward_kernel(counts, q_ref, k_ref, v_ref, bias_ref, o_ref, p_ref):
    comp_low = CM - counts[0]
    mem_low = CM + M - counts[1]
    for tile in range(SEG // TQ):
        cols = slice(tile * TQ, (tile + 1) * TQ)
        seen = CM + M + (tile + 1) * TQ
        raw = times_transposed(k_ref[:seen, :], q_ref[cols, :]) * SCALE
        blocks = seen // PW
        raw = (
            raw.reshape(blocks, PW, TQ) + bias_ref[0, :blocks, cols].reshape(blocks, 1, TQ)
        ).reshape(seen, TQ)
        key_pos = lax.broadcasted_iota(jnp.int32, (seen, TQ), 0)
        query_pos = CM + M + tile * TQ + lax.broadcasted_iota(jnp.int32, (seen, TQ), 1)
        low = jnp.where(key_pos < CM, comp_low, jnp.where(key_pos < CM + M, mem_low, 0))
        scores = jnp.where((key_pos >= low) & (key_pos <= query_pos), raw, MASKED)
        top = jnp.max(scores, axis=0, keepdims=True)
        expanded = jnp.exp(scores - top)
        total = jnp.sum(expanded, axis=0, keepdims=True)
        attention = (expanded * (1.0 / total)).astype(BF)
        p_ref[0, :seen, cols] = attention
        if seen < KR:
            p_ref[0, seen:, cols] = jnp.zeros((KR - seen, TQ), BF)
        mixed = contract_rows(v_ref[:seen, :], attention)
        o_ref[cols, :] = mixed.T.astype(BF)


def attention_forward(counts, queries, keys, values, bias):
    return pl.pallas_call(
        attention_forward_kernel,
        grid=(OH,),
        in_specs=[
            pl.BlockSpec(memory_space=pltpu.SMEM),
            pl.BlockSpec((SEG, HD), lambda h: (0, h)),
            pl.BlockSpec((KR, HD), lambda h: (0, h)),
            pl.BlockSpec((KR, HD), lambda h: (0, h)),
            pl.BlockSpec((1, NB, SEG), lambda h: (h, 0, 0)),
        ],
        out_specs=[
            pl.BlockSpec((SEG, HD), lambda h: (0, h)),
            pl.BlockSpec((1, KR, SEG), lambda h: (h, 0, 0)),
        ],
        out_shape=[
            jax.ShapeDtypeStruct((SEG, HALF), BF),
            jax.ShapeDtypeStruct((OH, KR, SEG), BF),
        ],
        cost_estimate=pl.CostEstimate(flops=1 << 20, bytes_accessed=1 << 16, transcendentals=0),
        name="attention_forward",
    )(counts, queries, keys, values, bias)


def half_rows(ref, half, rows):
    pieces = SEG // (2 * rows)
    return jnp.concatenate(
        [ref[pl.ds(pl.multiple_of((2 * i + half) * rows, rows), rows), :] for i in range(pieces)]
    )


def attention_backward_kernel(
    core, p_ref, q_ref, k_ref, v_ref, mine_ref, twin_ref, out_ref,
    dq_ref, dkv_ref, columns_ref, sums_ref, ds_ref, g_ref, *, rows,
):
    weight = out_ref[...]
    for half, branch in ((core[0], mine_ref), (1 - core[0], twin_ref)):
        part = times_transposed(branch[...], weight).astype(BF)
        for i in range(SEG // (2 * rows)):
            start = pl.multiple_of((2 * i + half) * rows, rows)
            g_ref[pl.ds(start, rows), :] = part[i * rows : (i + 1) * rows]
    query_sum = jnp.zeros((1, HD), F32)
    block_sums = []
    for tile in range(SEG // TQ):
        cols = slice(tile * TQ, (tile + 1) * TQ)
        seen = CM + M + (tile + 1) * TQ
        blocks = seen // PW
        attention = p_ref[0, :seen, cols].astype(F32)
        grad_attention = times_transposed(v_ref[:seen, :], g_ref[cols, :])
        inner = jnp.sum(attention * grad_attention, axis=0, keepdims=True)
        grad_scores = (attention * (grad_attention - inner)).astype(BF)
        ds_ref[:seen, cols] = grad_scores
        block_sum = jnp.sum(grad_scores.astype(F32).reshape(blocks, PW, TQ), axis=1)
        if seen < KR:
            ds_ref[seen:, cols] = jnp.zeros((KR - seen, TQ), BF)
            block_sum = jnp.concatenate([block_sum, jnp.zeros((NB - blocks, TQ), F32)], axis=0)
        block_sums.append(block_sum)
        grad_query = contract_rows(k_ref[:seen, :], grad_scores) * SCALE
        grad_query = grad_query.T.astype(BF)
        dq_ref[cols, :] = grad_query
        query_sum += jnp.sum(grad_query.astype(F32), axis=0, keepdims=True)
    grad_key = (matmul(ds_ref[...], q_ref[...]) * SCALE).astype(BF)
    dkv_ref[:, :HD] = grad_key
    grad_value = matmul(p_ref[0], g_ref[...]).astype(BF)
    dkv_ref[:, HD:] = grad_value
    columns_ref[...] = jnp.concatenate(
        [
            query_sum,
            jnp.sum(grad_key.astype(F32), axis=0, keepdims=True),
            jnp.sum(grad_value.astype(F32), axis=0, keepdims=True),
            jnp.zeros((1, HD), F32),
        ],
        axis=0,
    )
    picks = (
        lax.broadcasted_iota(jnp.int32, (SEG, HD), 0) // PW
        == lax.broadcasted_iota(jnp.int32, (SEG, HD), 1)
    ).astype(F32)
    sums_ref[0] = jnp.dot(
        jnp.concatenate(block_sums, axis=1), picks,
        precision=lax.Precision.HIGHEST, preferred_element_type=F32,
    )


def attention_backward(core, attention, queries, keys, values, mine, twin, attn_weights, rows):
    rows_of = lambda n: pl.BlockSpec((n, HD), lambda h, core: (0, h))
    whole = pl.BlockSpec((SEG // 2, D), lambda h, core: (0, 0))
    return pl.pallas_call(
        functools.partial(attention_backward_kernel, rows=rows),
        grid_spec=pltpu.PrefetchScalarGridSpec(
            num_scalar_prefetch=1,
            grid=(OH,),
            in_specs=[
                pl.BlockSpec((1, KR, SEG), lambda h, core: (h, 0, 0)),
                rows_of(SEG),
                rows_of(KR),
                rows_of(KR),
                whole,
                whole,
                pl.BlockSpec((HD, D), lambda h, core: (3 * H + OH * core[0] + h, 0)),
            ],
            out_specs=[
                rows_of(SEG),
                pl.BlockSpec((KR, 2 * HD), lambda h, core: (0, h)),
                rows_of(4),
                pl.BlockSpec((1, NB, HD), lambda h, core: (h, 0, 0)),
            ],
            scratch_shapes=[pltpu.VMEM((KR, SEG), BF), pltpu.VMEM((SEG, HD), BF)],
        ),
        out_shape=[
            jax.ShapeDtypeStruct((SEG, HALF), BF),
            jax.ShapeDtypeStruct((KR, 2 * HALF), BF),
            jax.ShapeDtypeStruct((4, HALF), F32),
            jax.ShapeDtypeStruct((OH, NB, HD), F32),
        ],
        cost_estimate=pl.CostEstimate(flops=1 << 20, bytes_accessed=1 << 16, transcendentals=0),
        name="attention_backward",
    )(core, attention, queries, keys, values, mine, twin, attn_weights)


def residual_kernel(
    core, mine_ref, twin_ref, out_ref, seg_ref, gain_ref, shift_ref, residual_ref, in_ref, *, rows
):
    half = core[0]
    total = seg_ref[...].astype(F32)
    for which, ref in ((half, mine_ref), (1 - half, twin_ref)):
        weight = out_ref[pl.ds(pl.multiple_of(which * HALF, HALF), HALF), :]
        total += matmul(half_rows(ref, half, rows), weight)
    residual_ref[...] = total
    hat, _ = statistics(total)
    in_ref[...] = (hat * gain_ref[...] + shift_ref[...]).astype(BF)


def residual_norm(core, mine, twin, attn_weights, segment, gain, shift, rows):
    count = SEG // 2
    whole = lambda a, b: pl.BlockSpec((a, b), lambda i, core: (0, 0))
    return pl.pallas_call(
        functools.partial(residual_kernel, rows=rows),
        grid_spec=pltpu.PrefetchScalarGridSpec(
            num_scalar_prefetch=1,
            grid=(1,),
            in_specs=[
                whole(SEG, HALF),
                whole(SEG, HALF),
                pl.BlockSpec((D, D), lambda i, core: (3, 0)),
                whole(count, D),
                whole(1, D),
                whole(1, D),
            ],
            out_specs=[whole(count, D), whole(count, D)],
        ),
        out_shape=[
            jax.ShapeDtypeStruct((count, D), F32),
            jax.ShapeDtypeStruct((count, D), BF),
        ],
        cost_estimate=pl.CostEstimate(flops=1 << 20, bytes_accessed=1 << 16, transcendentals=0),
        name="residual_norm",
    )(core, mine, twin, attn_weights, segment, gain.reshape(1, D), shift.reshape(1, D))


def norm_backward_kernel(
    residual_ref, own_ref, came_ref, gy_ref, gain_ref, grad_ref, branch_ref, sums_ref
):
    hat, inverse = statistics(residual_ref[...])
    grad = own_ref[...] + came_ref[...].astype(F32)
    sums_ref[...] = jnp.concatenate(
        [jnp.sum(grad * hat, axis=0, keepdims=True), jnp.sum(grad, axis=0, keepdims=True)], axis=0
    )
    total = gy_ref[...].astype(F32) + norm_pull(hat, inverse, grad * gain_ref[...])
    grad_ref[...] = total
    branch_ref[...] = total.astype(BF)


def norm_backward(residual, own, came, gy, gain):
    count = residual.shape[0]
    return pl.pallas_call(
        norm_backward_kernel,
        out_shape=[
            jax.ShapeDtypeStruct((count, D), F32),
            jax.ShapeDtypeStruct((count, D), BF),
            jax.ShapeDtypeStruct((2, D), F32),
        ],
        cost_estimate=pl.CostEstimate(flops=1 << 20, bytes_accessed=1 << 16, transcendentals=0),
        name="norm_backward",
    )(residual, own, came, gy, gain.reshape(1, D))


def owners_kernel(
    seg_ref, keep_ref, came_ref, grad_ref, gain_ref, residual_ref, part_ref, next_ref, bias_ref,
    out_ref,
):
    layers, _, rows, _ = out_ref.shape
    result = residual_ref[...] + (part_ref[...] + next_ref[...].astype(F32) + bias_ref[...])
    out_ref[:, 0] = result.astype(BF).reshape(layers, rows, D)
    hat, inverse = statistics(seg_ref[...].astype(F32))
    cotangent = (keep_ref[...] + came_ref[...].astype(F32)) * gain_ref[...]
    result = grad_ref[...] + norm_pull(hat, inverse, cotangent)
    out_ref[:, 1] = result.astype(BF).reshape(layers, rows, D)


def owners_rows(segment, keep, came, grad, gain, residual, part, part_next, bias, layers):
    count = segment.shape[0]
    return pl.pallas_call(
        owners_kernel,
        out_shape=jax.ShapeDtypeStruct((layers, 2, count // layers, D), BF),
        cost_estimate=pl.CostEstimate(flops=1 << 20, bytes_accessed=1 << 16, transcendentals=0),
        name="owners_rows",
    )(
        segment, keep, came, grad, gain.reshape(1, D), residual, part, part_next,
        bias.reshape(1, D),
    )


def normed_kernel(
    core, dq_ref, dkv_ref, wq_ref, wk_ref, wv_ref, keep_ref, send_ref, all_ref, *, rows
):
    total = times_transposed(dq_ref[...], wq_ref[...])
    both = dkv_ref[CM + M :, :]
    weight = []
    for head in range(OH):
        span = slice(head * HD, (head + 1) * HD)
        weight += [wk_ref[:, span], wv_ref[:, span]]
    total += times_transposed(both, jnp.concatenate(weight, axis=1))
    all_ref[...] = total
    send_ref[...] = half_rows(all_ref, 1 - core[0], rows).astype(BF)
    keep_ref[...] = half_rows(all_ref, core[0], rows)


def normed_gradient(core, dq, dkv, weights, rows):
    width = D // 4
    whole = lambda n: pl.BlockSpec((n, HALF), lambda i, core: (0, 0))
    block = lambda m: pl.BlockSpec((width, HALF), lambda i, core: (i + 4 * m, 0))
    out = pl.BlockSpec((SEG // 2, width), lambda i, core: (0, i))
    return pl.pallas_call(
        functools.partial(normed_kernel, rows=rows),
        grid_spec=pltpu.PrefetchScalarGridSpec(
            num_scalar_prefetch=1,
            grid=(4,),
            in_specs=[
                whole(SEG),
                pl.BlockSpec((KR, 2 * HALF), lambda i, core: (0, 0)),
                block(0), block(1), block(2),
            ],
            out_specs=[out, out],
            scratch_shapes=[pltpu.VMEM((SEG, width), F32)],
        ),
        out_shape=[
            jax.ShapeDtypeStruct((SEG // 2, D), F32),
            jax.ShapeDtypeStruct((SEG // 2, D), BF),
        ],
        cost_estimate=pl.CostEstimate(flops=1 << 20, bytes_accessed=1 << 16, transcendentals=0),
        name="normed_gradient",
    )(core, dq, dkv, weights, weights, weights)


def feed_forward_kernel(packed, added, *refs):
    x_ref, gy_ref = refs[:2]
    if packed:
        bias_ref, weights_ref = refs[2:4]
        rest = refs[4:]
        pieces, _, height, hidden = weights_ref.shape
        up = weights_ref[:, 0].reshape(pieces * height, hidden)
        down = weights_ref[:, 1].reshape(pieces * height, hidden)
    else:
        bias_ref, up_ref, down_ref = refs[2:5]
        rest = refs[5:]
        up, down = up_ref[...], down_ref[...]
    if added:
        prev_part, prev_grad = rest[:2]
        rest = rest[2:]
    part_ref, grad_ref, act_ref, pre_ref, sum_ref = rest
    rows = x_ref[...]
    hidden = matmul(rows, up) + bias_ref[...]
    normal = 0.5 * (1.0 + lax.erf(hidden * math.sqrt(0.5)))
    slope = normal + hidden * jnp.exp(-0.5 * hidden * hidden) * (1.0 / math.sqrt(2.0 * math.pi))
    activated = (hidden * normal).astype(BF)
    act_ref[...] = activated
    grad_hidden = times_transposed(gy_ref[...], down)
    grad_pre = (grad_hidden * slope).astype(BF)
    pre_ref[...] = grad_pre
    grad = times_transposed(grad_pre, up)
    part = matmul(activated, down)
    if added:
        grad = grad + prev_grad[...]
        part = part + prev_part[...]
    grad_ref[...] = grad.astype(grad_ref.dtype)
    part_ref[...] = part.astype(part_ref.dtype)
    sum_ref[...] = jnp.sum(grad_pre.astype(F32), axis=0, keepdims=True)


def feed_forward(rows, gy, bias, weights, previous, dtype):
    height = rows.shape[0]
    hidden = bias.shape[-1]
    packed = len(weights) == 1
    operands = [rows, gy, bias, *weights, *previous]
    return pl.pallas_call(
        functools.partial(feed_forward_kernel, packed, bool(previous)),
        out_shape=[
            jax.ShapeDtypeStruct((height, D), dtype),
            jax.ShapeDtypeStruct((height, D), dtype),
            jax.ShapeDtypeStruct((height, hidden), BF),
            jax.ShapeDtypeStruct((height, hidden), BF),
            jax.ShapeDtypeStruct((1, hidden), F32),
        ],
        compiler_params=pltpu.CompilerParams(vmem_limit_bytes=60 << 20),
        cost_estimate=pl.CostEstimate(
            flops=32 * height * D * hidden,
            bytes_accessed=32 << 20,
            transcendentals=8 * height * hidden,
        ),
        name="feed_forward",
    )(*operands)


def weight_kernel(place, *refs, by_high, send):
    lefts, rights, refs = refs[:4], refs[4:8], refs[8:]
    bit = place[0] if not send else 1 - place[0]
    step = pl.program_id(0)

    def columns(ref):
        starts = [pl.multiple_of((4 * step + 2 * p + bit) * HD, HD) for p in range(2)]
        return jnp.concatenate([ref[:, pl.ds(start, HD)] for start in starts], axis=1)

    for which in range(2):
        total = contract_rows(columns(lefts[2 * which]), rights[2 * which][...])
        total += contract_rows(columns(lefts[2 * which + 1]), rights[2 * which + 1][...])
        if send:
            refs[0][:, which] = total.astype(BF).reshape(2, HD, total.shape[1])
            continue
        came_ref, keep_ref, send_ref = refs
        for low in range(2):
            piece = total[low * HD : (low + 1) * HD] + came_ref[low, which].astype(F32)
            piece = piece.astype(BF)
            if by_high:

                @pl.when(step == place[1])
                def _():
                    keep_ref[low, which] = piece

                @pl.when(step != place[1])
                def _():
                    send_ref[low, which] = piece
            else:

                @pl.when(low == place[2])
                def _():
                    keep_ref[step, which] = piece

                @pl.when(low != place[2])
                def _():
                    send_ref[step, which] = piece


def place_piece(keep_ref, send_ref, where, piece, value, place, by_high):
    high, low = piece // 2, piece % 2
    bit, other, mine = (high, low, place[1]) if by_high else (low, high, place[2])

    @pl.when(bit == mine)
    def _():
        keep_ref[(other, *where)] = value

    @pl.when(bit != mine)
    def _():
        send_ref[(other, *where)] = value


def weight_gradients(place, left, right, by_high, came=None):
    count, hidden = right[0].shape
    pieces = D // HD // 2
    send = came is None
    each = pl.BlockSpec((pieces // 2, 2, HD, hidden), lambda i, place: (i, 0, 0, 0))
    half = pl.BlockSpec((pieces // 2, 2, HD, hidden), lambda i, place: (0, 0, 0, 0))
    shape = lambda n: jax.ShapeDtypeStruct((n, 2, HD, hidden), BF)
    return pl.pallas_call(
        functools.partial(weight_kernel, by_high=by_high, send=send),
        grid_spec=pltpu.PrefetchScalarGridSpec(
            num_scalar_prefetch=1,
            grid=(2,),
            in_specs=[pl.BlockSpec((count, D), lambda i, place: (0, 0))] * 4
            + [pl.BlockSpec((count, hidden), lambda i, place: (0, 0))] * 4
            + ([] if send else [each]),
            out_specs=each if send else [half, half],
        ),
        out_shape=shape(pieces) if send else [shape(pieces // 2)] * 2,
        cost_estimate=pl.CostEstimate(flops=1 << 20, bytes_accessed=1 << 16, transcendentals=0),
        name="weight_send" if send else "weight_keep",
    )(place, *left, *right, *(() if send else (came,)))


def projection_kernel(
    place, core, normed_ref, mixed_mine, mixed_twin, dq_ref, dkv_ref,
    branch_mine, branch_twin, wq_ref, wk_ref, wv_ref, columns_ref,
    low_keep, low_send, high_keep, high_send, vector_ref, mixed_ref, *, rows,
):
    step = pl.program_id(0)
    half = core[0]
    gain = jnp.zeros((HALF, HD), F32)
    shift = jnp.zeros((HALF, HD), F32)

    def store(which, total):
        value = total.astype(BF).reshape(HALF // HD, HD, HALF)

        @pl.when(step == 0)
        def _():
            place_piece(low_keep, low_send, (), which, value, place, False)

        @pl.when(step == 1)
        def _():
            place_piece(high_keep, high_send, (), which, value, place, True)

    both = contract_rows(normed_ref[...], dkv_ref[...])
    heads = [both[:, i * HD : (i + 1) * HD] for i in range(2 * OH)]
    for which, (total, weight_ref) in enumerate(
        (
            (contract_rows(normed_ref[CM + M :, :], dq_ref[...]), wq_ref),
            (jnp.concatenate(heads[::2], axis=1), wk_ref),
            (jnp.concatenate(heads[1::2], axis=1), wv_ref),
        )
    ):
        store(which, total)
        weight = weight_ref[...].astype(F32)
        sums = columns_ref[which : which + 1, :]
        for part in range(OH):
            span = slice(part * HD, (part + 1) * HD)
            gain += weight[:, span] * total[:, span]
            shift += weight[:, span] * sums[:, span]

    @pl.when(step == half)
    def _():
        mixed_ref[...] = mixed_mine[...]

    @pl.when(step != half)
    def _():
        mixed_ref[...] = mixed_twin[...]

    total = contract_rows(half_rows(mixed_ref, half, rows), branch_mine[...])
    total += contract_rows(half_rows(mixed_ref, 1 - half, rows), branch_twin[...])
    store(3, total)
    vector_ref[...] = jnp.zeros(vector_ref.shape, F32)
    for part in range(HALF // HD):
        span = slice(part * HD, (part + 1) * HD)
        vector_ref[0:1, span] = jnp.sum(gain[span].T, axis=0, keepdims=True)
        vector_ref[1:2, span] = jnp.sum(shift[span].T, axis=0, keepdims=True)


def projection_gradients(
    place, core, normed, mixed_mine, mixed_twin, dq, dkv, branch_mine, branch_twin,
    weights, columns, rows,
):
    whole = lambda n: pl.BlockSpec((n, HALF), lambda i, *_: (0, 0))
    branch = pl.BlockSpec((SEG // 2, HALF), lambda i, place, core: (0, core[0]))
    weight = lambda m: pl.BlockSpec((HALF, HALF), lambda i, *_: (i + 2 * m, 0))
    out = pl.BlockSpec((2, HALF // HD, HD, HALF), lambda i, *_: (0, 0, 0, 0))
    shape = jax.ShapeDtypeStruct((2, HALF // HD, HD, HALF), BF)
    return pl.pallas_call(
        functools.partial(projection_kernel, rows=rows),
        grid_spec=pltpu.PrefetchScalarGridSpec(
            num_scalar_prefetch=2,
            grid=(2,),
            in_specs=[
                pl.BlockSpec((KR, HALF), lambda i, *_: (0, i)),
                whole(SEG), whole(SEG),
                whole(SEG),
                pl.BlockSpec((KR, 2 * HALF), lambda i, *_: (0, 0)),
                branch, branch,
                weight(0), weight(1), weight(2),
                whole(4),
            ],
            out_specs=[out] * 4 + [pl.BlockSpec((8, HALF), lambda i, *_: (0, i))],
            scratch_shapes=[pltpu.VMEM((SEG, HALF), BF)],
        ),
        out_shape=[shape] * 4 + [jax.ShapeDtypeStruct((8, D), F32)],
        cost_estimate=pl.CostEstimate(flops=1 << 20, bytes_accessed=1 << 16, transcendentals=0),
        name="projection_gradients",
    )(
        place, core, normed, mixed_mine, mixed_twin, dq, dkv, branch_mine, branch_twin,
        weights, weights, weights, columns,
    )


def on_device(
    seg_input,
    memory,
    compressed,
    mem_fill,
    comp_fill,
    attn_gain,
    attn_shift,
    attn_weights,
    rel_table,
    ffn_gain,
    ffn_shift,
    w_up,
    b_up,
    w_down,
    b_down,
    conv_weight,
    conv_bias,
    out_grad,
    comp_grad,
):
    streams = lax.axis_size("dp")
    layers = lax.axis_size("ffn")
    stream = lax.axis_index("dp")
    layer = lax.axis_index("ffn")
    core = stream % 2
    micros = seg_input.shape[0]
    seg_rows, mem_rows, comp_rows = seg_input.shape[2], memory.shape[2], compressed.shape[2]
    hidden_local = w_up.shape[1]
    twins = [(i, i ^ 1) for i in range(streams)]
    first = core == 0
    which_core = core.reshape(1).astype(jnp.int32)

    def swap(value):
        return lax.ppermute(value, "dp", twins)

    def by_core(mine, other, axis):
        return jnp.where(
            first, jnp.stack([mine, other], axis=axis), jnp.stack([other, mine], axis=axis)
        )

    def halves(value):
        split = value.reshape(micros, 2, value.shape[1] // 2, D)
        return (
            lax.dynamic_index_in_dim(split, core, 1, keepdims=False),
            lax.dynamic_index_in_dim(split, 1 - core, 1, keepdims=False),
        )

    seg, mem, comp = seg_input[:, 0], memory[:, 0], compressed[:, 0]
    gy_own, comp_cot = out_grad[:, 0], comp_grad[:, 0]

    kept, sent = zip(*[halves(x) for x in (comp, mem, seg, gy_own)])
    came = swap(jnp.concatenate(sent, axis=1))
    kept = jnp.concatenate(kept, axis=1)
    pairs = by_core(kept, came, 1).reshape(2 * micros, -1, D)
    hc, hm, hs = comp_rows // 2, mem_rows // 2, seg_rows // 2
    pairs, mem, comp_cot, b_up, comp_fill, gy_own = together(
        pairs, mem, comp_cot, b_up, comp_fill, gy_own
    )
    source_rows = hc + hm + hs
    source = lax.all_to_all(pairs, "ffn", split_axis=0, concat_axis=0, tiled=True)

    fills = jnp.concatenate([comp_fill, mem_fill], axis=1).astype(F32)
    twin_fills = swap(fills)
    pair_micro, pair_core = layer // 2, layer % 2
    counts = lax.dynamic_index_in_dim(
        jnp.where(pair_core == core, fills, twin_fills), pair_micro, 0, keepdims=False
    ).astype(jnp.int32)

    memory_pos = layer * mem_rows + jnp.arange(mem_rows, dtype=jnp.int32)
    alive = memory_pos[None, :] >= M - mem_fill
    flat = jnp.where(alive[:, :, None], mem, jnp.zeros_like(mem))
    flat = flat.reshape(micros * (mem_rows // 3), 3 * D)
    new_compressed = (matmul(flat, conv_weight) + conv_bias).astype(BF)
    new_compressed = new_compressed.reshape(micros, 1, mem_rows // 3, D)
    cot_rows = comp_cot.reshape(-1, D)
    conv_part = contract_rows(flat, cot_rows).astype(BF)
    conv_rows = lax.psum_scatter(conv_part, "dp", scatter_dimension=0, tiled=True)
    conv_bias_part = jnp.sum(cot_rows.astype(F32), axis=0)
    down_bias_part = jnp.sum(gy_own.astype(F32), axis=(0, 1))

    own_columns = lax.dynamic_slice(attn_weights, (0, core * HALF), (3 * D, HALF))
    table = lax.dynamic_slice(rel_table, (core * OH, 0), (OH, NB))
    query_blocks = SEG // PW
    first_block = (CM + M) // PW
    extended = jnp.concatenate([jnp.full((OH, query_blocks - 1), MASKED, F32), table], axis=1)
    offset = first_block + query_blocks - 1
    bias = jnp.stack(
        [extended[:, offset - b : offset - b + query_blocks] for b in range(NB)], axis=1
    )
    bias = jnp.broadcast_to(bias[..., None], (OH, NB, query_blocks, PW)).reshape(OH, NB, SEG)

    height = D // streams
    across = [(i, i ^ 2) for i in range(layers)]
    beside = [(i, i ^ 1) for i in range(layers)]
    carried = jnp.stack(
        [lax.dynamic_slice(w, (stream * height, 0), (height, hidden_local)) for w in (w_up, w_down)]
    )
    far_bias = lax.ppermute(b_up.reshape(1, hidden_local), "ffn", across)

    (
        source, new_compressed, carried, counts, bias, far_bias, own_columns,
        conv_bias_part, down_bias_part,
    ) = together(
        source, new_compressed, carried, counts, bias, far_bias, own_columns,
        conv_bias_part, down_bias_part,
    )
    w_query, w_key, w_value = own_columns[:D], own_columns[D : 2 * D], own_columns[2 * D :]
    gy_half = source[:, source_rows:].reshape(layers * hs, D)
    gy_next = lax.ppermute(gy_half, "ffn", beside)
    carried = lax.ppermute(carried, "ffn", across)

    normed_half = norm_rows(source, source_rows, attn_gain, attn_shift, conv_part)
    normed_pair = by_core(normed_half, swap(normed_half), 0)
    normed_pair = normed_pair.reshape(2, layers, source_rows, D)
    sections = []
    start = 0
    for count in (hc, hm, hs):
        piece = normed_pair[:, :, start : start + count]
        sections.append(piece.transpose(1, 0, 2, 3).reshape(2 * layers * count, D))
        start += count
    (normed,) = together(jnp.concatenate(sections, axis=0))
    queries = matmul(normed[CM + M :], w_query).astype(BF)
    keys = matmul(normed, w_key).astype(BF)
    values = matmul(normed, w_value).astype(BF)

    mixed_own, attention = attention_forward(counts, queries, keys, values, bias)
    mixed_own, carried, gy_next, conv_rows = together(mixed_own, carried, gy_next, conv_rows)
    far_weights = lax.all_gather(carried[None], "dp", axis=0, tiled=True)
    mixed_twin = swap(mixed_own)
    segment = source[:, hc + hm : source_rows].reshape(layers * hs, D)
    residual, ffn_in = residual_norm(
        which_core, mixed_own, mixed_twin, attn_weights, segment, ffn_gain, ffn_shift, hs
    )

    bits = streams.bit_length() - 1
    inner = bits - 3

    def partners(bit):
        return [(i, i ^ (1 << bit)) for i in range(streams)]

    def combine(stay, goes, bit):
        other = lax.ppermute(goes, "dp", partners(bit))
        return (stay.astype(F32) + other.astype(F32)).astype(BF)

    def reduce_over(value, axes, order):
        axes = list(axes)
        for bit in order:
            axis = axes.index(bit)
            mine = (stream >> bit) & 1
            stay = lax.dynamic_index_in_dim(value, mine, axis, keepdims=False)
            goes = lax.dynamic_index_in_dim(value, 1 - mine, axis, keepdims=False)
            value = combine(stay, goes, bit)
            axes.pop(axis)
        return value

    bias_row = b_up.reshape(1, hidden_local)
    ffn_next = lax.ppermute(ffn_in, "ffn", beside)
    near = (w_up, w_down)
    own_part, own_grad, act_own, pre_own, sum_a = feed_forward(
        ffn_in, gy_half, bias_row, near, (), F32
    )
    next_part, next_grad, act_next, pre_next, sum_b = feed_forward(
        ffn_next, gy_next, bias_row, near, (), F32
    )
    top, next_top = bits - 1, bits - 2
    lower = list(range(inner - 1, -1, -1))
    place = jnp.stack([(stream >> bit) & 1 for bit in (inner, top, next_top)]).astype(jnp.int32)
    left = (ffn_in, ffn_next, gy_half, gy_next)
    right = (pre_own, pre_next, act_own, act_next)
    near_part = weight_gradients(place, left, right, True)
    far_weights, near_part, conv_rows = together(far_weights, near_part, conv_rows)
    conv_rows = lax.psum_scatter(conv_rows, "ffn", scatter_dimension=0, tiled=True)
    near_part = lax.ppermute(near_part, "dp", partners(inner))
    far = (far_weights,)
    next_part, next_grad, far_act_next, far_pre_next, sum_c = feed_forward(
        ffn_next, gy_next, far_bias, far, (next_part, next_grad), BF
    )
    grad_came = lax.ppermute(next_grad, "ffn", beside)
    part_came = lax.ppermute(next_part, "ffn", beside)
    own_part, own_grad, far_act_own, far_pre_own, sum_d = feed_forward(
        ffn_in, gy_half, far_bias, far, (own_part, own_grad), F32
    )
    near_keep, near_send = weight_gradients(place, left, right, True, near_part)
    grad_came, near_send = together(grad_came, near_send)
    up_bias_part = sum_a + sum_b
    far_bias_part = sum_c + sum_d

    grad_residual, branch, norm_sums = norm_backward(
        residual, own_grad, grad_came, gy_half, ffn_gain
    )
    branch, far_pre_own = together(branch, far_pre_own)
    branch_twin = swap(branch)
    right = (far_pre_own, far_pre_next, far_act_own, far_act_next)
    far_part = weight_gradients(place, left, right, False)
    far_part = lax.ppermute(far_part, "dp", partners(inner))
    near_sum = combine(near_keep, near_send, top)
    branch_twin, conv_rows = together(branch_twin, conv_rows)
    conv_grad = lax.all_gather(conv_rows, ("dp", "ffn"), axis=0, tiled=True).astype(F32)

    grad_query, grad_keys, columns, sums = attention_backward(
        which_core, attention, queries, keys, values, branch, branch_twin, attn_weights, hs
    )
    grad_query, part_came, far_part = together(grad_query, part_came, far_part)
    far_keep, far_send = weight_gradients(place, left, right, False, far_part)
    grad_keys, far_send = together(grad_keys, far_send)
    normed_keep, normed_send = normed_gradient(
        which_core, grad_query, grad_keys, own_columns, hs
    )
    normed_came = swap(normed_send)
    low_keep, low_send, high_keep, high_send, vectors = projection_gradients(
        place, which_core, normed, mixed_own, mixed_twin, grad_query, grad_keys,
        branch, branch_twin, own_columns, columns, hs,
    )
    far_sum = combine(far_keep, far_send, next_top)
    vectors, far_sum, near_sum, grad_residual = together(
        vectors, far_sum, near_sum, grad_residual
    )
    shift_part = vectors[1]
    gain_part = (vectors[0] - attn_shift * shift_part) / attn_gain

    rows_out = owners_rows(
        segment, normed_keep, normed_came, grad_residual, attn_gain, residual, own_part,
        part_came, b_down, layers,
    )
    split = (2, 2) + (2,) * inner + (height, hidden_local)
    far_sum = reduce_over(far_sum.reshape(split), [top, None] + lower, [top] + lower)
    rows_out = lax.all_to_all(rows_out, "ffn", split_axis=0, concat_axis=0, tiled=True)
    low = combine(low_keep, low_send, next_top)
    high = combine(high_keep, high_send, top)
    high, rows_out = together(high, rows_out)

    tile_sums = sums[:, :, :query_blocks]
    distance = (
        first_block
        + jnp.arange(query_blocks, dtype=jnp.int32)[None, :]
        - jnp.arange(NB, dtype=jnp.int32)[:, None]
    )
    one_hot = (distance[:, :, None] == jnp.arange(NB, dtype=jnp.int32)).astype(F32)
    table_part = jnp.einsum("hkq,kqn->hn", tile_sums, one_hot, precision=lax.Precision.HIGHEST)
    table_row = lax.dynamic_update_slice(jnp.zeros((H, NB), F32), table_part, (core * OH, 0))
    table_row = jnp.pad(table_row.reshape(-1), (0, D - H * NB))
    up_bias_rows = lax.dynamic_update_slice(
        jnp.zeros((layers, hidden_local), F32), up_bias_part, (layer, 0)
    )
    up_bias_rows = lax.dynamic_update_slice(up_bias_rows, far_bias_part, (layer ^ 2, 0))
    up_bias_rows = up_bias_rows.reshape(-1, D)
    up_bias_count = up_bias_rows.shape[0]
    small = jnp.concatenate(
        [
            jnp.stack(
                [gain_part, shift_part, norm_sums[0], norm_sums[1], down_bias_part,
                 conv_bias_part, table_row]
            ),
            up_bias_rows,
        ]
    )
    for bit in range(bits):
        small = small + lax.ppermute(small, "dp", partners(bit))
    low, far_sum, small = together(low, far_sum, small)
    for pairs_of in (beside, across):
        small = small + lax.ppermute(small, "ffn", pairs_of)
    far_came = lax.ppermute(far_sum, "ffn", across)
    rows_out = rows_out.reshape(micros, 2, 2, hs, D)
    rows_stay = lax.dynamic_index_in_dim(rows_out, core, 1, keepdims=False)
    rows_came = swap(lax.dynamic_index_in_dim(rows_out, 1 - core, 1, keepdims=False))
    rows_out = by_core(rows_stay, rows_came, 2).reshape(micros, 2, 2 * hs, D)
    layer_out = rows_out[:, :1]
    seg_grad = rows_out[:, 1:].astype(F32)

    near_sum = near_sum.reshape(split)
    near_sum = reduce_over(near_sum, [next_top, None] + lower, [next_top] + lower)

    piece_rows = 4 * D // (streams * layers)
    split = (2,) + (2,) * inner + (layers, piece_rows, HALF)
    rest = [bit for bit in lower if bit > 0]
    low = low.reshape(split)
    low = reduce_over(low, [top] + lower, [top] + rest)
    high = high.reshape(split)
    high = reduce_over(high, [next_top] + lower, [next_top] + rest)
    both = jnp.stack([low, high])
    if inner:
        both = reduce_over(both, [inner], [inner])
    both, far_came, small, conv_grad = together(both, far_came, small, conv_grad)
    both = both.reshape(2, 2, 2, piece_rows, HALF)
    for bit, pairs_of in ((0, beside), (1, across)):
        mine = (layer >> bit) & 1
        axis = 2 - bit
        stay = lax.dynamic_index_in_dim(both, mine, axis, keepdims=False)
        goes = lax.dynamic_index_in_dim(both, 1 - mine, axis, keepdims=False)
        both = stay.astype(F32) + lax.ppermute(goes, "ffn", pairs_of).astype(F32)
        both = both.astype(BF)
    weight_sum = near_sum.astype(F32) + far_came.astype(F32)
    up_grad = weight_sum[0]
    down_grad = weight_sum[1].T
    stay = lax.dynamic_index_in_dim(both, core, 0, keepdims=False)
    other = swap(lax.dynamic_index_in_dim(both, 1 - core, 0, keepdims=False))
    attn_weights_grad = by_core(stay, other, 1).reshape(piece_rows, D).astype(F32)

    return (
        layer_out,
        new_compressed,
        seg_grad,
        small[0],
        small[1],
        attn_weights_grad,
        small[6, : H * NB].reshape(H, NB),
        small[2],
        small[3],
        up_grad,
        small[7 : 7 + up_bias_count].reshape(-1),
        down_grad,
        small[4],
        conv_grad,
        small[5],
    )


def solution(mesh):
    return jax.shard_map(
        on_device,
        mesh=mesh,
        in_specs=(
            P(None, "dp", "ffn", None),
            P(None, "dp", "ffn", None),
            P(None, "dp", "ffn", None),
            P(None, "dp"),
            P(None, "dp"),
            P(),
            P(),
            P(),
            P(),
            P(),
            P(),
            P(None, "ffn"),
            P("ffn"),
            P("ffn", None),
            P(),
            P(),
            P(),
            P(None, "dp", "ffn", None),
            P(None, "dp", "ffn", None),
        ),
        out_specs=(
            P(None, "dp", "ffn", None),
            P(None, "dp", "ffn", None),
            P(None, "dp", "ffn", None),
            P(),
            P(),
            P(("dp", "ffn"), None),
            P(),
            P(),
            P(),
            P("dp", "ffn"),
            P(),
            P("ffn", "dp"),
            P(),
            P(),
            P(),
        ),
        check_vma=False,
    )
```

```python
import functools
import math

import jax
import jax.numpy as jnp
from jax import lax
from jax.experimental import pallas as pl
from jax.experimental.pallas import tpu as pltpu
from jax.sharding import PartitionSpec as P

D = 1024
H = 8
HD = 128
SEG = 512
M = 384
CM = 512
PW = 64
KR = 1408
NB = 22
OH = 4
TQ = 128
HALF = OH * HD
EPSILON = 1e-05
MASKED = -1e30
SCALE = HD ** (-0.5)
BF = jnp.bfloat16
F32 = jnp.float32


def statistics(rows_in):
    centre = jnp.mean(rows_in, axis=-1, keepdims=True)
    centred = rows_in - centre
    variance = jnp.mean(centred * centred, axis=-1, keepdims=True)
    inverse = lax.rsqrt(variance + EPSILON)
    return centred * inverse, inverse


def matmul(left, right):
    return jnp.dot(left, right, preferred_element_type=F32)


def contract_rows(left, right):
    return lax.dot_general(left, right, (((0,), (0,)), ((), ())), preferred_element_type=F32)


def times_transposed(left, right):
    return lax.dot_general(left, right, (((1,), (1,)), ((), ())), preferred_element_type=F32)


def together(*values):
    return lax.optimization_barrier(values)


def norm_pull(xhat, inverse, scaled):
    mean_a = jnp.mean(scaled, axis=-1, keepdims=True)
    mean_b = jnp.mean(scaled * xhat, axis=-1, keepdims=True)
    return (scaled - mean_a - xhat * mean_b) * inverse


def norm_kernel(x_ref, gain_ref, shift_ref, _, out_ref):
    hat, _ = statistics(x_ref[0].astype(F32))
    out_ref[0] = (hat * gain_ref[...] + shift_ref[...]).astype(BF)


def norm_rows(rows, count, gain, shift, earlier):
    layers = rows.shape[0]
    return pl.pallas_call(
        norm_kernel,
        grid=(layers,),
        in_specs=[
            pl.BlockSpec((1, count, D), lambda i: (i, 0, 0)),
            pl.BlockSpec((1, D), lambda i: (0, 0)),
            pl.BlockSpec((1, D), lambda i: (0, 0)),
            pl.BlockSpec(memory_space=pl.ANY),
        ],
        out_specs=pl.BlockSpec((1, count, D), lambda i: (i, 0, 0)),
        out_shape=jax.ShapeDtypeStruct((layers, count, D), BF),
        cost_estimate=pl.CostEstimate(flops=1 << 20, bytes_accessed=1 << 16, transcendentals=0),
        name="norm_rows",
    )(rows, gain.reshape(1, D), shift.reshape(1, D), earlier)


def attention_forward_kernel(counts, q_ref, k_ref, v_ref, bias_ref, o_ref, p_ref):
    comp_low = CM - counts[0]
    mem_low = CM + M - counts[1]
    for tile in range(SEG // TQ):
        cols = slice(tile * TQ, (tile + 1) * TQ)
        seen = CM + M + (tile + 1) * TQ
        raw = times_transposed(k_ref[:seen, :], q_ref[cols, :]) * SCALE
        blocks = seen // PW
        raw = (
            raw.reshape(blocks, PW, TQ) + bias_ref[0, :blocks, cols].reshape(blocks, 1, TQ)
        ).reshape(seen, TQ)
        key_pos = lax.broadcasted_iota(jnp.int32, (seen, TQ), 0)
        query_pos = CM + M + tile * TQ + lax.broadcasted_iota(jnp.int32, (seen, TQ), 1)
        low = jnp.where(key_pos < CM, comp_low, jnp.where(key_pos < CM + M, mem_low, 0))
        scores = jnp.where((key_pos >= low) & (key_pos <= query_pos), raw, MASKED)
        top = jnp.max(scores, axis=0, keepdims=True)
        expanded = jnp.exp(scores - top)
        total = jnp.sum(expanded, axis=0, keepdims=True)
        attention = (expanded * (1.0 / total)).astype(BF)
        p_ref[0, :seen, cols] = attention
        if seen < KR:
            p_ref[0, seen:, cols] = jnp.zeros((KR - seen, TQ), BF)
        mixed = contract_rows(v_ref[:seen, :], attention)
        o_ref[cols, :] = mixed.T.astype(BF)


def attention_forward(counts, queries, keys, values, bias):
    return pl.pallas_call(
        attention_forward_kernel,
        grid=(OH,),
        in_specs=[
            pl.BlockSpec(memory_space=pltpu.SMEM),
            pl.BlockSpec((SEG, HD), lambda h: (0, h)),
            pl.BlockSpec((KR, HD), lambda h: (0, h)),
            pl.BlockSpec((KR, HD), lambda h: (0, h)),
            pl.BlockSpec((1, NB, SEG), lambda h: (h, 0, 0)),
        ],
        out_specs=[
            pl.BlockSpec((SEG, HD), lambda h: (0, h)),
            pl.BlockSpec((1, KR, SEG), lambda h: (h, 0, 0)),
        ],
        out_shape=[
            jax.ShapeDtypeStruct((SEG, HALF), BF),
            jax.ShapeDtypeStruct((OH, KR, SEG), BF),
        ],
        cost_estimate=pl.CostEstimate(flops=1 << 20, bytes_accessed=1 << 16, transcendentals=0),
        name="attention_forward",
    )(counts, queries, keys, values, bias)


def half_rows(ref, half, rows):
    pieces = SEG // (2 * rows)
    return jnp.concatenate(
        [ref[pl.ds(pl.multiple_of((2 * i + half) * rows, rows), rows), :] for i in range(pieces)]
    )


def attention_backward_kernel(
    core, p_ref, q_ref, k_ref, v_ref, mine_ref, twin_ref, out_ref,
    dq_ref, dkv_ref, columns_ref, sums_ref, ds_ref, g_ref, *, rows,
):
    weight = out_ref[...]
    for half, branch in ((core[0], mine_ref), (1 - core[0], twin_ref)):
        part = times_transposed(branch[...], weight).astype(BF)
        for i in range(SEG // (2 * rows)):
            start = pl.multiple_of((2 * i + half) * rows, rows)
            g_ref[pl.ds(start, rows), :] = part[i * rows : (i + 1) * rows]
    query_sum = jnp.zeros((1, HD), F32)
    block_sums = []
    for tile in range(SEG // TQ):
        cols = slice(tile * TQ, (tile + 1) * TQ)
        seen = CM + M + (tile + 1) * TQ
        blocks = seen // PW
        attention = p_ref[0, :seen, cols].astype(F32)
        grad_attention = times_transposed(v_ref[:seen, :], g_ref[cols, :])
        inner = jnp.sum(attention * grad_attention, axis=0, keepdims=True)
        grad_scores = (attention * (grad_attention - inner)).astype(BF)
        ds_ref[:seen, cols] = grad_scores
        block_sum = jnp.sum(grad_scores.astype(F32).reshape(blocks, PW, TQ), axis=1)
        if seen < KR:
            ds_ref[seen:, cols] = jnp.zeros((KR - seen, TQ), BF)
            block_sum = jnp.concatenate([block_sum, jnp.zeros((NB - blocks, TQ), F32)], axis=0)
        block_sums.append(block_sum)
        grad_query = contract_rows(k_ref[:seen, :], grad_scores) * SCALE
        grad_query = grad_query.T.astype(BF)
        dq_ref[cols, :] = grad_query
        query_sum += jnp.sum(grad_query.astype(F32), axis=0, keepdims=True)
    grad_key = (matmul(ds_ref[...], q_ref[...]) * SCALE).astype(BF)
    dkv_ref[:, :HD] = grad_key
    grad_value = matmul(p_ref[0], g_ref[...]).astype(BF)
    dkv_ref[:, HD:] = grad_value
    columns_ref[...] = jnp.concatenate(
        [
            query_sum,
            jnp.sum(grad_key.astype(F32), axis=0, keepdims=True),
            jnp.sum(grad_value.astype(F32), axis=0, keepdims=True),
            jnp.zeros((1, HD), F32),
        ],
        axis=0,
    )
    picks = (
        lax.broadcasted_iota(jnp.int32, (SEG, HD), 0) // PW
        == lax.broadcasted_iota(jnp.int32, (SEG, HD), 1)
    ).astype(F32)
    sums_ref[0] = jnp.dot(
        jnp.concatenate(block_sums, axis=1), picks,
        precision=lax.Precision.HIGHEST, preferred_element_type=F32,
    )


def attention_backward(core, attention, queries, keys, values, mine, twin, attn_weights, rows):
    rows_of = lambda n: pl.BlockSpec((n, HD), lambda h, core: (0, h))
    whole = pl.BlockSpec((SEG // 2, D), lambda h, core: (0, 0))
    return pl.pallas_call(
        functools.partial(attention_backward_kernel, rows=rows),
        grid_spec=pltpu.PrefetchScalarGridSpec(
            num_scalar_prefetch=1,
            grid=(OH,),
            in_specs=[
                pl.BlockSpec((1, KR, SEG), lambda h, core: (h, 0, 0)),
                rows_of(SEG),
                rows_of(KR),
                rows_of(KR),
                whole,
                whole,
                pl.BlockSpec((HD, D), lambda h, core: (3 * H + OH * core[0] + h, 0)),
            ],
            out_specs=[
                rows_of(SEG),
                pl.BlockSpec((KR, 2 * HD), lambda h, core: (0, h)),
                rows_of(4),
                pl.BlockSpec((1, NB, HD), lambda h, core: (h, 0, 0)),
            ],
            scratch_shapes=[pltpu.VMEM((KR, SEG), BF), pltpu.VMEM((SEG, HD), BF)],
        ),
        out_shape=[
            jax.ShapeDtypeStruct((SEG, HALF), BF),
            jax.ShapeDtypeStruct((KR, 2 * HALF), BF),
            jax.ShapeDtypeStruct((4, HALF), F32),
            jax.ShapeDtypeStruct((OH, NB, HD), F32),
        ],
        cost_estimate=pl.CostEstimate(flops=1 << 20, bytes_accessed=1 << 16, transcendentals=0),
        name="attention_backward",
    )(core, attention, queries, keys, values, mine, twin, attn_weights)


def residual_kernel(
    core, mine_ref, twin_ref, out_ref, seg_ref, gain_ref, shift_ref, residual_ref, in_ref, *, rows
):
    half = core[0]
    total = seg_ref[...].astype(F32)
    for which, ref in ((half, mine_ref), (1 - half, twin_ref)):
        weight = out_ref[pl.ds(pl.multiple_of(which * HALF, HALF), HALF), :]
        total += matmul(half_rows(ref, half, rows), weight)
    residual_ref[...] = total
    hat, _ = statistics(total)
    in_ref[...] = (hat * gain_ref[...] + shift_ref[...]).astype(BF)


def residual_norm(core, mine, twin, attn_weights, segment, gain, shift, rows):
    count = SEG // 2
    whole = lambda a, b: pl.BlockSpec((a, b), lambda i, core: (0, 0))
    return pl.pallas_call(
        functools.partial(residual_kernel, rows=rows),
        grid_spec=pltpu.PrefetchScalarGridSpec(
            num_scalar_prefetch=1,
            grid=(1,),
            in_specs=[
                whole(SEG, HALF),
                whole(SEG, HALF),
                pl.BlockSpec((D, D), lambda i, core: (3, 0)),
                whole(count, D),
                whole(1, D),
                whole(1, D),
            ],
            out_specs=[whole(count, D), whole(count, D)],
        ),
        out_shape=[
            jax.ShapeDtypeStruct((count, D), F32),
            jax.ShapeDtypeStruct((count, D), BF),
        ],
        cost_estimate=pl.CostEstimate(flops=1 << 20, bytes_accessed=1 << 16, transcendentals=0),
        name="residual_norm",
    )(core, mine, twin, attn_weights, segment, gain.reshape(1, D), shift.reshape(1, D))


def norm_backward_kernel(
    residual_ref, own_ref, came_ref, gy_ref, gain_ref, grad_ref, branch_ref, sums_ref
):
    step = residual_ref.shape[0] // 4
    sums_ref[...] = jnp.zeros(sums_ref.shape, F32)

    @pl.loop(0, 4)
    def _(i):
        rows = pl.ds(pl.multiple_of(i * step, step), step)
        hat, inverse = statistics(residual_ref[rows, :])
        grad = own_ref[rows, :] + came_ref[rows, :].astype(F32)
        sums_ref[0:1, :] += jnp.sum(grad * hat, axis=0, keepdims=True)
        sums_ref[1:2, :] += jnp.sum(grad, axis=0, keepdims=True)
        total = gy_ref[rows, :].astype(F32) + norm_pull(hat, inverse, grad * gain_ref[...])
        grad_ref[rows, :] = total
        branch_ref[rows, :] = total.astype(BF)


def norm_backward(residual, own, came, gy, gain):
    count = residual.shape[0]
    return pl.pallas_call(
        norm_backward_kernel,
        out_shape=[
            jax.ShapeDtypeStruct((count, D), F32),
            jax.ShapeDtypeStruct((count, D), BF),
            jax.ShapeDtypeStruct((2, D), F32),
        ],
        cost_estimate=pl.CostEstimate(flops=1 << 20, bytes_accessed=1 << 16, transcendentals=0),
        name="norm_backward",
    )(residual, own, came, gy, gain.reshape(1, D))


def owners_kernel(
    seg_ref, keep_ref, came_ref, grad_ref, gain_ref, residual_ref, part_ref, next_ref, bias_ref,
    out_ref,
):
    layers, _, step, _ = out_ref.shape

    @pl.loop(0, layers)
    def _(i):
        rows = pl.ds(pl.multiple_of(i * step, step), step)
        result = residual_ref[rows, :] + (
            part_ref[rows, :] + next_ref[rows, :].astype(F32) + bias_ref[...]
        )
        out_ref[i, 0] = result.astype(BF)
        hat, inverse = statistics(seg_ref[rows, :].astype(F32))
        cotangent = (keep_ref[rows, :] + came_ref[rows, :].astype(F32)) * gain_ref[...]
        result = grad_ref[rows, :] + norm_pull(hat, inverse, cotangent)
        out_ref[i, 1] = result.astype(BF)


def owners_rows(segment, keep, came, grad, gain, residual, part, part_next, bias, layers):
    count = segment.shape[0]
    return pl.pallas_call(
        owners_kernel,
        out_shape=jax.ShapeDtypeStruct((layers, 2, count // layers, D), BF),
        cost_estimate=pl.CostEstimate(flops=1 << 20, bytes_accessed=1 << 16, transcendentals=0),
        name="owners_rows",
    )(
        segment, keep, came, grad, gain.reshape(1, D), residual, part, part_next,
        bias.reshape(1, D),
    )


def normed_kernel(
    core, dq_ref, dkv_ref, wq_ref, wk_ref, wv_ref, keep_ref, send_ref, all_ref, *, rows
):
    total = times_transposed(dq_ref[...], wq_ref[...])
    both = dkv_ref[CM + M :, :]
    weight = []
    for head in range(OH):
        span = slice(head * HD, (head + 1) * HD)
        weight += [wk_ref[:, span], wv_ref[:, span]]
    total += times_transposed(both, jnp.concatenate(weight, axis=1))
    all_ref[...] = total
    send_ref[...] = half_rows(all_ref, 1 - core[0], rows).astype(BF)
    keep_ref[...] = half_rows(all_ref, core[0], rows)


def normed_gradient(core, dq, dkv, weights, rows):
    width = D // 4
    whole = lambda n: pl.BlockSpec((n, HALF), lambda i, core: (0, 0))
    block = lambda m: pl.BlockSpec((width, HALF), lambda i, core: (i + 4 * m, 0))
    out = pl.BlockSpec((SEG // 2, width), lambda i, core: (0, i))
    return pl.pallas_call(
        functools.partial(normed_kernel, rows=rows),
        grid_spec=pltpu.PrefetchScalarGridSpec(
            num_scalar_prefetch=1,
            grid=(4,),
            in_specs=[
                whole(SEG),
                pl.BlockSpec((KR, 2 * HALF), lambda i, core: (0, 0)),
                block(0), block(1), block(2),
            ],
            out_specs=[out, out],
            scratch_shapes=[pltpu.VMEM((SEG, width), F32)],
        ),
        out_shape=[
            jax.ShapeDtypeStruct((SEG // 2, D), F32),
            jax.ShapeDtypeStruct((SEG // 2, D), BF),
        ],
        cost_estimate=pl.CostEstimate(flops=1 << 20, bytes_accessed=1 << 16, transcendentals=0),
        name="normed_gradient",
    )(core, dq, dkv, weights, weights, weights)


def feed_forward_kernel(packed, added, *refs):
    x_ref, gy_ref = refs[:2]
    if packed:
        bias_ref, weights_ref = refs[2:4]
        rest = refs[4:]
        pieces, _, height, hidden = weights_ref.shape
        up = weights_ref[:, 0].reshape(pieces * height, hidden)
        down = weights_ref[:, 1].reshape(pieces * height, hidden)
    else:
        bias_ref, up_ref, down_ref = refs[2:5]
        rest = refs[5:]
        up, down = up_ref[...], down_ref[...]
    if added:
        prev_part, prev_grad = rest[:2]
        rest = rest[2:]
    part_ref, grad_ref, act_ref, pre_ref, sum_ref, *low_refs = rest
    rows = x_ref[...]
    hidden = matmul(rows, up) + bias_ref[...]
    normal = 0.5 * (1.0 + lax.erf(hidden * math.sqrt(0.5)))
    slope = normal + hidden * jnp.exp(-0.5 * hidden * hidden) * (1.0 / math.sqrt(2.0 * math.pi))
    activated = (hidden * normal).astype(BF)
    act_ref[...] = activated
    grad_hidden = times_transposed(gy_ref[...], down)
    grad_pre = (grad_hidden * slope).astype(BF)
    pre_ref[...] = grad_pre
    grad = times_transposed(grad_pre, up)
    part = matmul(activated, down)
    if added:
        grad = grad + prev_grad[...]
        part = part + prev_part[...]
        low_refs[0][...] = part.astype(BF)
        low_refs[1][...] = grad.astype(BF)
    grad_ref[...] = grad
    part_ref[...] = part
    sum_ref[...] = jnp.sum(grad_pre.astype(F32), axis=0, keepdims=True)


def feed_forward(rows, gy, bias, weights, previous):
    height = rows.shape[0]
    hidden = bias.shape[-1]
    packed = len(weights) == 1
    operands = [rows, gy, bias, *weights, *previous]
    return pl.pallas_call(
        functools.partial(feed_forward_kernel, packed, bool(previous)),
        out_shape=[
            jax.ShapeDtypeStruct((height, D), F32),
            jax.ShapeDtypeStruct((height, D), F32),
            jax.ShapeDtypeStruct((height, hidden), BF),
            jax.ShapeDtypeStruct((height, hidden), BF),
            jax.ShapeDtypeStruct((1, hidden), F32),
        ]
        + [jax.ShapeDtypeStruct((height, D), BF)] * len(previous),
        compiler_params=pltpu.CompilerParams(vmem_limit_bytes=60 << 20),
        cost_estimate=pl.CostEstimate(
            flops=32 * height * D * hidden,
            bytes_accessed=32 << 20,
            transcendentals=8 * height * hidden,
        ),
        name="feed_forward",
    )(*operands)


def weight_kernel(place, *refs, by_high, send):
    lefts, rights, refs = refs[:4], refs[4:8], refs[8:]
    bit = place[0] if not send else 1 - place[0]
    step = pl.program_id(0)

    def columns(ref):
        starts = [pl.multiple_of((4 * step + 2 * p + bit) * HD, HD) for p in range(2)]
        return jnp.concatenate([ref[:, pl.ds(start, HD)] for start in starts], axis=1)

    for which in range(2):
        total = contract_rows(columns(lefts[2 * which]), rights[2 * which][...])
        total += contract_rows(columns(lefts[2 * which + 1]), rights[2 * which + 1][...])
        if send:
            refs[0][:, which] = total.astype(BF).reshape(2, HD, total.shape[1])
            continue
        came_ref, keep_ref, send_ref = refs
        for low in range(2):
            piece = total[low * HD : (low + 1) * HD] + came_ref[low, which].astype(F32)
            piece = piece.astype(BF)
            if by_high:

                @pl.when(step == place[1])
                def _():
                    keep_ref[low, which] = piece

                @pl.when(step != place[1])
                def _():
                    send_ref[low, which] = piece
            else:

                @pl.when(low == place[2])
                def _():
                    keep_ref[step, which] = piece

                @pl.when(low != place[2])
                def _():
                    send_ref[step, which] = piece


def place_piece(keep_ref, send_ref, where, piece, value, place, by_high):
    high, low = piece // 2, piece % 2
    bit, other, mine = (high, low, place[1]) if by_high else (low, high, place[2])

    @pl.when(bit == mine)
    def _():
        keep_ref[(other, *where)] = value

    @pl.when(bit != mine)
    def _():
        send_ref[(other, *where)] = value


def weight_gradients(place, left, right, by_high, came=None):
    count, hidden = right[0].shape
    pieces = D // HD // 2
    send = came is None
    each = pl.BlockSpec((pieces // 2, 2, HD, hidden), lambda i, place: (i, 0, 0, 0))
    half = pl.BlockSpec((pieces // 2, 2, HD, hidden), lambda i, place: (0, 0, 0, 0))
    shape = lambda n: jax.ShapeDtypeStruct((n, 2, HD, hidden), BF)
    return pl.pallas_call(
        functools.partial(weight_kernel, by_high=by_high, send=send),
        grid_spec=pltpu.PrefetchScalarGridSpec(
            num_scalar_prefetch=1,
            grid=(2,),
            in_specs=[pl.BlockSpec((count, D), lambda i, place: (0, 0))] * 4
            + [pl.BlockSpec((count, hidden), lambda i, place: (0, 0))] * 4
            + ([] if send else [each]),
            out_specs=each if send else [half, half],
        ),
        out_shape=shape(pieces) if send else [shape(pieces // 2)] * 2,
        cost_estimate=pl.CostEstimate(flops=1 << 20, bytes_accessed=1 << 16, transcendentals=0),
        name="weight_send" if send else "weight_keep",
    )(place, *left, *right, *(() if send else (came,)))


def projection_kernel(
    place, core, normed_ref, mixed_mine, mixed_twin, dq_ref, dkv_ref,
    branch_mine, branch_twin, wq_ref, wk_ref, wv_ref, columns_ref,
    low_keep, low_send, high_keep, high_send, vector_ref, mixed_ref, *, rows,
):
    step = pl.program_id(0)
    half_steps = pl.num_programs(0) // 2
    half = core[0]
    gain = jnp.zeros((HD, HD), F32)
    shift = jnp.zeros((HD, HD), F32)
    mixed_ref[...] = jnp.where(
        step // half_steps == half, mixed_mine[...].astype(F32), mixed_twin[...].astype(F32)
    )
    out = contract_rows(half_rows(mixed_ref, half, rows).astype(BF), branch_mine[...])
    out += contract_rows(half_rows(mixed_ref, 1 - half, rows).astype(BF), branch_twin[...])
    both = contract_rows(normed_ref[...], dkv_ref[...])
    heads = [both[:, i * HD : (i + 1) * HD] for i in range(2 * OH)]
    totals = [
        contract_rows(normed_ref[CM + M :, :], dq_ref[...]),
        jnp.concatenate(heads[::2], axis=1),
        jnp.concatenate(heads[1::2], axis=1),
        out,
    ]
    for which, weight_ref in enumerate((wq_ref, wk_ref, wv_ref)):
        weight = weight_ref[...].astype(F32)
        sums = columns_ref[which : which + 1, :]
        for part in range(OH):
            span = slice(part * HD, (part + 1) * HD)
            gain += weight[:, span] * totals[which][:, span]
            shift += weight[:, span] * sums[:, span]
    vector_ref[...] = jnp.concatenate(
        [
            jnp.sum(gain.T, axis=0, keepdims=True),
            jnp.sum(shift.T, axis=0, keepdims=True),
            jnp.zeros((6, HD), F32),
        ],
        axis=0,
    )
    values = [total.astype(BF) for total in totals]

    @pl.when(step < half_steps)
    def _():
        for which, value in enumerate(values):
            place_piece(low_keep, low_send, (0,), which, value, place, False)

    @pl.when(step >= half_steps)
    def _():
        for which, value in enumerate(values):
            place_piece(high_keep, high_send, (0,), which, value, place, True)


def projection_gradients(
    place, core, normed, mixed_mine, mixed_twin, dq, dkv, branch_mine, branch_twin,
    weights, columns, rows,
):
    steps = D // HD
    half = steps // 2
    whole = lambda n: pl.BlockSpec((n, HALF), lambda i, *_: (0, 0))
    head = pl.BlockSpec((SEG, HD), lambda i, *_: (0, i % OH))
    branch = pl.BlockSpec((SEG // 2, HALF), lambda i, place, core: (0, core[0]))
    weight = lambda m: pl.BlockSpec((HD, HALF), lambda i, *_: (i + m * steps, 0))
    first = pl.BlockSpec((2, 1, HD, HALF), lambda i, *_: (0, jnp.minimum(i, half - 1), 0, 0))
    last = pl.BlockSpec((2, 1, HD, HALF), lambda i, *_: (0, jnp.maximum(i - half, 0), 0, 0))
    shape = jax.ShapeDtypeStruct((2, half, HD, HALF), BF)
    return pl.pallas_call(
        functools.partial(projection_kernel, rows=rows),
        grid_spec=pltpu.PrefetchScalarGridSpec(
            num_scalar_prefetch=2,
            grid=(steps,),
            in_specs=[
                pl.BlockSpec((KR, HD), lambda i, *_: (0, i)),
                head, head,
                whole(SEG),
                pl.BlockSpec((KR, 2 * HALF), lambda i, *_: (0, 0)),
                branch, branch,
                weight(0), weight(1), weight(2),
                whole(4),
            ],
            out_specs=[first, first, last, last, pl.BlockSpec((8, HD), lambda i, *_: (0, i))],
            scratch_shapes=[pltpu.VMEM((SEG, HD), F32)],
        ),
        out_shape=[shape] * 4 + [jax.ShapeDtypeStruct((8, D), F32)],
        cost_estimate=pl.CostEstimate(flops=1 << 20, bytes_accessed=1 << 16, transcendentals=0),
        name="projection_gradients",
    )(
        place, core, normed, mixed_mine, mixed_twin, dq, dkv, branch_mine, branch_twin,
        weights, weights, weights, columns,
    )


def on_device(
    seg_input,
    memory,
    compressed,
    mem_fill,
    comp_fill,
    attn_gain,
    attn_shift,
    attn_weights,
    rel_table,
    ffn_gain,
    ffn_shift,
    w_up,
    b_up,
    w_down,
    b_down,
    conv_weight,
    conv_bias,
    out_grad,
    comp_grad,
):
    streams = lax.axis_size("dp")
    layers = lax.axis_size("ffn")
    stream = lax.axis_index("dp")
    layer = lax.axis_index("ffn")
    core = stream % 2
    micros = seg_input.shape[0]
    seg_rows, mem_rows, comp_rows = seg_input.shape[2], memory.shape[2], compressed.shape[2]
    hidden_local = w_up.shape[1]
    twins = [(i, i ^ 1) for i in range(streams)]
    first = core == 0
    which_core = core.reshape(1).astype(jnp.int32)

    def swap(value):
        return lax.ppermute(value, "dp", twins)

    def by_core(mine, other, axis):
        return jnp.where(
            first, jnp.stack([mine, other], axis=axis), jnp.stack([other, mine], axis=axis)
        )

    def halves(value):
        split = value.reshape(micros, 2, value.shape[1] // 2, D)
        return (
            lax.dynamic_index_in_dim(split, core, 1, keepdims=False),
            lax.dynamic_index_in_dim(split, 1 - core, 1, keepdims=False),
        )

    seg, mem, comp = seg_input[:, 0], memory[:, 0], compressed[:, 0]
    gy_own, comp_cot = out_grad[:, 0], comp_grad[:, 0]

    kept, sent = zip(*[halves(x) for x in (comp, mem, seg, gy_own)])
    came = swap(jnp.concatenate(sent, axis=1))
    kept = jnp.concatenate(kept, axis=1)
    pairs = by_core(kept, came, 1).reshape(2 * micros, -1, D)
    hc, hm, hs = comp_rows // 2, mem_rows // 2, seg_rows // 2
    pairs, mem, comp_cot, b_up, comp_fill, gy_own = together(
        pairs, mem, comp_cot, b_up, comp_fill, gy_own
    )
    source_rows = hc + hm + hs
    source = lax.all_to_all(pairs, "ffn", split_axis=0, concat_axis=0, tiled=True)

    fills = jnp.concatenate([comp_fill, mem_fill], axis=1).astype(F32)
    twin_fills = swap(fills)
    pair_micro, pair_core = layer // 2, layer % 2
    counts = lax.dynamic_index_in_dim(
        jnp.where(pair_core == core, fills, twin_fills), pair_micro, 0, keepdims=False
    ).astype(jnp.int32)

    memory_pos = layer * mem_rows + jnp.arange(mem_rows, dtype=jnp.int32)
    alive = memory_pos[None, :] >= M - mem_fill
    flat = jnp.where(alive[:, :, None], mem, jnp.zeros_like(mem))
    flat = flat.reshape(micros * (mem_rows // 3), 3 * D)
    new_compressed = (matmul(flat, conv_weight) + conv_bias).astype(BF)
    new_compressed = new_compressed.reshape(micros, 1, mem_rows // 3, D)
    cot_rows = comp_cot.reshape(-1, D)
    conv_part = contract_rows(flat, cot_rows).astype(BF)
    conv_rows = lax.psum_scatter(conv_part, "dp", scatter_dimension=0, tiled=True)
    conv_bias_part = jnp.sum(cot_rows.astype(F32), axis=0)
    down_bias_part = jnp.sum(gy_own.astype(F32), axis=(0, 1))

    own_columns = lax.dynamic_slice(attn_weights, (0, core * HALF), (3 * D, HALF))
    table = lax.dynamic_slice(rel_table, (core * OH, 0), (OH, NB))
    query_blocks = SEG // PW
    first_block = (CM + M) // PW
    extended = jnp.concatenate([jnp.full((OH, query_blocks - 1), MASKED, F32), table], axis=1)
    offset = first_block + query_blocks - 1
    bias = jnp.stack(
        [extended[:, offset - b : offset - b + query_blocks] for b in range(NB)], axis=1
    )
    bias = jnp.broadcast_to(bias[..., None], (OH, NB, query_blocks, PW)).reshape(OH, NB, SEG)

    height = D // streams
    across = [(i, i ^ 2) for i in range(layers)]
    beside = [(i, i ^ 1) for i in range(layers)]
    carried = jnp.stack(
        [lax.dynamic_slice(w, (stream * height, 0), (height, hidden_local)) for w in (w_up, w_down)]
    )
    far_bias = lax.ppermute(b_up.reshape(1, hidden_local), "ffn", across)

    (
        source, new_compressed, carried, counts, bias, far_bias, own_columns,
        conv_bias_part, down_bias_part,
    ) = together(
        source, new_compressed, carried, counts, bias, far_bias, own_columns,
        conv_bias_part, down_bias_part,
    )
    w_query, w_key, w_value = own_columns[:D], own_columns[D : 2 * D], own_columns[2 * D :]
    gy_half = source[:, source_rows:].reshape(layers * hs, D)
    gy_next = lax.ppermute(gy_half, "ffn", beside)
    carried = lax.ppermute(carried, "ffn", across)

    normed_half = norm_rows(source, source_rows, attn_gain, attn_shift, conv_part)
    normed_pair = by_core(normed_half, swap(normed_half), 0)
    normed_pair = normed_pair.reshape(2, layers, source_rows, D)
    sections = []
    start = 0
    for count in (hc, hm, hs):
        piece = normed_pair[:, :, start : start + count]
        sections.append(piece.transpose(1, 0, 2, 3).reshape(2 * layers * count, D))
        start += count
    (normed,) = together(jnp.concatenate(sections, axis=0))
    queries = matmul(normed[CM + M :], w_query).astype(BF)
    keys = matmul(normed, w_key).astype(BF)
    values = matmul(normed, w_value).astype(BF)

    mixed_own, attention = attention_forward(counts, queries, keys, values, bias)
    mixed_own, carried, gy_next, conv_rows = together(mixed_own, carried, gy_next, conv_rows)
    far_weights = lax.all_gather(carried[None], "dp", axis=0, tiled=True)
    mixed_twin = swap(mixed_own)
    segment = source[:, hc + hm : source_rows].reshape(layers * hs, D)
    residual, ffn_in = residual_norm(
        which_core, mixed_own, mixed_twin, attn_weights, segment, ffn_gain, ffn_shift, hs
    )

    bits = streams.bit_length() - 1
    inner = bits - 3

    def partners(bit):
        return [(i, i ^ (1 << bit)) for i in range(streams)]

    def combine(stay, goes, bit):
        other = lax.ppermute(goes, "dp", partners(bit))
        return (stay.astype(F32) + other.astype(F32)).astype(BF)

    def reduce_over(value, axes, order):
        axes = list(axes)
        for bit in order:
            axis = axes.index(bit)
            mine = (stream >> bit) & 1
            stay = lax.dynamic_index_in_dim(value, mine, axis, keepdims=False)
            goes = lax.dynamic_index_in_dim(value, 1 - mine, axis, keepdims=False)
            value = combine(stay, goes, bit)
            axes.pop(axis)
        return value

    bias_row = b_up.reshape(1, hidden_local)
    ffn_next = lax.ppermute(ffn_in, "ffn", beside)
    near = (w_up, w_down)
    own_part, own_grad, act_own, pre_own, sum_a = feed_forward(
        ffn_in, gy_half, bias_row, near, ()
    )
    next_part, next_grad, act_next, pre_next, sum_b = feed_forward(
        ffn_next, gy_next, bias_row, near, ()
    )
    top, next_top = bits - 1, bits - 2
    lower = list(range(inner - 1, -1, -1))
    place = jnp.stack([(stream >> bit) & 1 for bit in (inner, top, next_top)]).astype(jnp.int32)
    left = (ffn_in, ffn_next, gy_half, gy_next)
    right = (pre_own, pre_next, act_own, act_next)
    near_part = weight_gradients(place, left, right, True)
    far_weights, near_part, conv_rows = together(far_weights, near_part, conv_rows)
    conv_rows = lax.psum_scatter(conv_rows, "ffn", scatter_dimension=0, tiled=True)
    near_part = lax.ppermute(near_part, "dp", partners(inner))
    far = (far_weights,)
    _, _, far_act_next, far_pre_next, sum_c, next_part, next_grad = feed_forward(
        ffn_next, gy_next, far_bias, far, (next_part, next_grad)
    )
    grad_came = lax.ppermute(next_grad, "ffn", beside)
    part_came = lax.ppermute(next_part, "ffn", beside)
    own_part, own_grad, far_act_own, far_pre_own, sum_d, *_ = feed_forward(
        ffn_in, gy_half, far_bias, far, (own_part, own_grad)
    )
    far_right = (far_pre_own, far_pre_next, far_act_own, far_act_next)
    far_part = weight_gradients(place, left, far_right, False)
    grad_came, far_part = together(grad_came, far_part)
    far_part = lax.ppermute(far_part, "dp", partners(inner))
    up_bias_part = sum_a + sum_b
    far_bias_part = sum_c + sum_d

    grad_residual, branch, norm_sums = norm_backward(
        residual, own_grad, grad_came, gy_half, ffn_gain
    )
    branch_twin = swap(branch)
    far_keep, far_send = weight_gradients(place, left, far_right, False, far_part)
    near_keep, near_send = weight_gradients(place, left, right, True, near_part)
    branch_twin, far_send, near_send, conv_rows = together(
        branch_twin, far_send, near_send, conv_rows
    )
    conv_grad = lax.all_gather(conv_rows, ("dp", "ffn"), axis=0, tiled=True).astype(F32)
    near_sum = combine(near_keep, near_send, top)
    far_sum = combine(far_keep, far_send, next_top)

    grad_query, grad_keys, columns, sums = attention_backward(
        which_core, attention, queries, keys, values, branch, branch_twin, attn_weights, hs
    )
    grad_query, part_came, far_sum = together(grad_query, part_came, far_sum)
    split = (2, 2) + (2,) * inner + (height, hidden_local)
    far_sum = reduce_over(far_sum.reshape(split), [top, None] + lower, [top] + lower)
    normed_keep, normed_send = normed_gradient(
        which_core, grad_query, grad_keys, own_columns, hs
    )
    normed_came = swap(normed_send)
    low_keep, low_send, high_keep, high_send, vectors = projection_gradients(
        place, which_core, normed, mixed_own, mixed_twin, grad_query, grad_keys,
        branch, branch_twin, own_columns, columns, hs,
    )
    vectors, near_sum, grad_residual = together(vectors, near_sum, grad_residual)
    shift_part = vectors[1]
    gain_part = (vectors[0] - attn_shift * shift_part) / attn_gain

    rows_out = owners_rows(
        segment, normed_keep, normed_came, grad_residual, attn_gain, residual, own_part,
        part_came, b_down, layers,
    )
    rows_out = lax.all_to_all(rows_out, "ffn", split_axis=0, concat_axis=0, tiled=True)
    low = combine(low_keep, low_send, next_top)
    high = combine(high_keep, high_send, top)
    high, rows_out = together(high, rows_out)

    tile_sums = sums[:, :, :query_blocks]
    distance = (
        first_block
        + jnp.arange(query_blocks, dtype=jnp.int32)[None, :]
        - jnp.arange(NB, dtype=jnp.int32)[:, None]
    )
    one_hot = (distance[:, :, None] == jnp.arange(NB, dtype=jnp.int32)).astype(F32)
    table_part = jnp.einsum("hkq,kqn->hn", tile_sums, one_hot, precision=lax.Precision.HIGHEST)
    table_row = lax.dynamic_update_slice(jnp.zeros((H, NB), F32), table_part, (core * OH, 0))
    table_row = jnp.pad(table_row.reshape(-1), (0, D - H * NB))
    up_bias_rows = lax.dynamic_update_slice(
        jnp.zeros((layers, hidden_local), F32), up_bias_part, (layer, 0)
    )
    up_bias_rows = lax.dynamic_update_slice(up_bias_rows, far_bias_part, (layer ^ 2, 0))
    up_bias_rows = up_bias_rows.reshape(-1, D)
    up_bias_count = up_bias_rows.shape[0]
    small = jnp.concatenate(
        [
            jnp.stack(
                [gain_part, shift_part, norm_sums[0], norm_sums[1], down_bias_part,
                 conv_bias_part, table_row]
            ),
            up_bias_rows,
        ]
    )
    low, far_sum = together(low, far_sum)
    far_came = lax.ppermute(far_sum, "ffn", across)
    for pairs_of in (beside, across):
        small = small + lax.ppermute(small, "ffn", pairs_of)
    rows_out = rows_out.reshape(micros, 2, 2, hs, D)
    rows_stay = lax.dynamic_index_in_dim(rows_out, core, 1, keepdims=False)
    rows_came = swap(lax.dynamic_index_in_dim(rows_out, 1 - core, 1, keepdims=False))
    rows_out = by_core(rows_stay, rows_came, 2).reshape(micros, 2, 2 * hs, D)
    layer_out = rows_out[:, :1]
    seg_grad = rows_out[:, 1:].astype(F32)

    near_sum = near_sum.reshape(split)
    near_sum = reduce_over(near_sum, [next_top, None] + lower, [next_top] + lower)

    piece_rows = 4 * D // (streams * layers)
    split = (2,) + (2,) * inner + (layers, piece_rows, HALF)
    rest = [bit for bit in lower if bit > 0]
    low = low.reshape(split)
    low = reduce_over(low, [top] + lower, [top] + rest)
    high = high.reshape(split)
    high = reduce_over(high, [next_top] + lower, [next_top] + rest)
    both = jnp.stack([low, high])
    if inner:
        both = reduce_over(both, [inner], [inner])
    both, small, conv_grad, far_came = together(both, small, conv_grad, far_came)
    both = both.reshape(2, 2, 2, piece_rows, HALF)
    for bit, pairs_of in ((0, beside), (1, across)):
        mine = (layer >> bit) & 1
        axis = 2 - bit
        stay = lax.dynamic_index_in_dim(both, mine, axis, keepdims=False)
        goes = lax.dynamic_index_in_dim(both, 1 - mine, axis, keepdims=False)
        came = lax.ppermute(goes, "ffn", pairs_of)
        for other in range(bits - 1) if bit == 0 else (bits - 1,):
            small = small + lax.ppermute(small, "dp", partners(other))
        came, small = together(came, small)
        both = (stay.astype(F32) + came.astype(F32)).astype(BF)
    weight_sum = near_sum.astype(F32) + far_came.astype(F32)
    up_grad = weight_sum[0]
    down_grad = weight_sum[1].T
    stay = lax.dynamic_index_in_dim(both, core, 0, keepdims=False)
    other = swap(lax.dynamic_index_in_dim(both, 1 - core, 0, keepdims=False))
    attn_weights_grad = by_core(stay, other, 1).reshape(piece_rows, D).astype(F32)

    return (
        layer_out,
        new_compressed,
        seg_grad,
        small[0],
        small[1],
        attn_weights_grad,
        small[6, : H * NB].reshape(H, NB),
        small[2],
        small[3],
        up_grad,
        small[7 : 7 + up_bias_count].reshape(-1),
        down_grad,
        small[4],
        conv_grad,
        small[5],
    )


def solution(mesh):
    return jax.shard_map(
        on_device,
        mesh=mesh,
        in_specs=(
            P(None, "dp", "ffn", None),
            P(None, "dp", "ffn", None),
            P(None, "dp", "ffn", None),
            P(None, "dp"),
            P(None, "dp"),
            P(),
            P(),
            P(),
            P(),
            P(),
            P(),
            P(None, "ffn"),
            P("ffn"),
            P("ffn", None),
            P(),
            P(),
            P(),
            P(None, "dp", "ffn", None),
            P(None, "dp", "ffn", None),
        ),
        out_specs=(
            P(None, "dp", "ffn", None),
            P(None, "dp", "ffn", None),
            P(None, "dp", "ffn", None),
            P(),
            P(),
            P(("dp", "ffn"), None),
            P(),
            P(),
            P(),
            P("dp", "ffn"),
            P(),
            P("ffn", "dp"),
            P(),
            P(),
            P(),
        ),
        check_vma=False,
    )
```
